32 devices in a mesh: fsdp: 8 (over y, x, core), ctx: 4 (over z).
Axes of the slice: x: 2, y: 2, z: 4, core: 2. Of those that a mesh axis runs over, the one named last changes fastest.
Arguments:
- tokens: bfloat16 [4096, 8192], P('fsdp'), may hold values from -12 to 12
- wq: bfloat16 [8192, 4096], P('fsdp', 'ctx'), may hold values from -0.0625 to 0.0625
- wo: bfloat16 [4096, 8192], P('ctx', 'fsdp'), may hold values from -1.5 to 1.5
- key_cache: bfloat16 [8192, 1024], P(('fsdp', 'ctx')), may hold values from -500 to 500, as said below
- value_cache: bfloat16 [8192, 1024], P(('fsdp', 'ctx')), may hold values from -6 to 6
- key_blocks: int32 [8, 4, 8], P('fsdp'), may hold values from 0 to 7, as said below
Outputs:
- mixed: bfloat16 [4096, 8192], P('fsdp', 'ctx')
The draws below stay inside these ranges and needn't reach their ends.
Inputs may be any that keep to these rules, and one draw needn't show every extreme that they name: `key_cache`: keys of order one; a sequence's first block may hold much larger ones. `key_blocks`: for query block b of sequence s, entries 0 to 2 name key blocks 8 - 4 + b - 2, 4 + b - 1 and 4 + b; entries 3 and 4 name blocks 0 and 1; the last 3 entries are random blocks. Counting the random entries of a sequence over its query blocks in order as t = 0, 1, ..., the t-th lies in blocks k * 2 to (k+1) * 2 - 1 with k = 1 + t mod (2); entries may repeat.
All inputs are finite; a program needn't handle non-finite values.
Results may differ from the reference program's by a relative error of at most 0.018.
Values may be sent and summed in bfloat16 or wider, within the bound.
A program may use at most 128 MiB of HBM per device.

```python
import jax
import jax.numpy as jnp
from jax import lax

D = 8192
HEADS = 32
KV_HEADS = 8
HEAD = 128
BLOCK = 128
QB = 4
RANDS = 3
BLK_DEV = 2
Q_LEN = 512
CACHE_BLOCKS = 8
KEYS = 1024
SEQS = 8
ROWS = 4096
N_CTX = 4


def draw_tokens(key, part):
    base = jnp.clip(jax.random.normal(key, (ROWS, D), jnp.float32), -6.0, 6.0)
    return base.astype(jnp.bfloat16)


def draw_key_cache(key, part):
    width = KV_HEADS * HEAD
    base = jnp.clip(jax.random.normal(key, (SEQS, KEYS, width), jnp.float32), -6.0, 6.0)
    return base.reshape(SEQS * KEYS, width).astype(jnp.bfloat16)


def draw_key_blocks(key, part):
    owner_count = CACHE_BLOCKS // BLK_DEV
    query_ids = jnp.arange(QB, dtype=jnp.int32)
    own_ids = CACHE_BLOCKS - QB + query_ids
    window = own_ids[:, None] + jnp.arange(-2, 1, dtype=jnp.int32)[None, :]
    anchors = jnp.broadcast_to(jnp.arange(2, dtype=jnp.int32)[None, :], (QB, 2))
    entry_ids = jnp.arange(QB * RANDS, dtype=jnp.int32).reshape(QB, RANDS)
    owner_ids = 1 + entry_ids % (owner_count - 2)
    offsets = jax.random.randint(key, (SEQS, QB, RANDS), 0, BLK_DEV, dtype=jnp.int32)
    randoms = owner_ids[None, :, :] * BLK_DEV + offsets
    fixed_part = jnp.concatenate([window, anchors], axis=1)
    listed = jnp.concatenate([jnp.broadcast_to(fixed_part[None, :, :], (SEQS, QB, 5)), randoms], axis=2)
    return listed.astype(jnp.int32)


def levels(stream_key, dims, cuts, least, high):
    def one(position, shards_of):
        draws = jax.random.uniform(jax.random.fold_in(jax.random.fold_in(stream_key, 6), position), (shards_of,), jnp.float32, least / len(cuts), high / len(cuts))
        return jnp.repeat(jnp.exp(draws), dims[position] // shards_of).reshape((-1,) + (1,) * (len(dims) - position - 1))

    gain = one(*cuts[0])
    for cut in cuts[1:]:
        gain = gain * one(*cut)
    return gain


def bell_draw(stream_key, dims, scale, limit, shards=(), held_as=jnp.bfloat16):
    gain = levels(stream_key, dims, shards, -0.22, 0.18) if shards else 1.0
    entries = jax.random.normal(stream_key, dims, jnp.float32) * scale * gain
    return jnp.minimum(jnp.maximum(entries, -limit), limit).astype(held_as)


def setup_inputs(seed: int = 0) -> dict:
    key_list = jax.random.split(jax.random.key(seed), 7)
    return {
        "tokens": draw_tokens(jax.random.fold_in(key_list[6], 71), 0),
        "wq": bell_draw(key_list[1], (D, HEADS * HEAD), D ** -0.5, 0.0625, ((0, 8), (1, 4))),
        "wo": bell_draw(key_list[2], (HEADS * HEAD, D), (HEAD // 8) ** -0.5, 1.5, ((0, 4), (1, 8))),
        "key_cache": draw_key_cache(jax.random.fold_in(key_list[6], 71), 0),
        "value_cache": bell_draw(key_list[4], (SEQS * KEYS, KV_HEADS * HEAD), 1.0, 6.0, ((0, 32),)),
        "key_blocks": draw_key_blocks(jax.random.fold_in(key_list[6], 71), 0),
    }


rope_base = 1000000.0


def rotate(vectors, positions):
    half_width = vectors.shape[-1] // 2
    frequency = rope_base ** (-(jnp.arange(half_width, dtype=jnp.float32) * 2.0) / vectors.shape[-1])
    angles = positions.astype(jnp.float32)[:, None] * frequency[None, :]
    cosine_table = jnp.cos(angles)[:, None, :]
    sine_table = jnp.sin(angles)[:, None, :]
    front_half = vectors[..., :half_width]
    back_half = vectors[..., half_width:]
    return jnp.concatenate([front_half * cosine_table - back_half * sine_table, back_half * cosine_table + front_half * sine_table], axis=-1)


def reference(tokens, wq, wo, key_cache, value_cache, key_blocks):
    group_size = HEADS // KV_HEADS
    positions = (KEYS - Q_LEN) + jnp.arange(Q_LEN, dtype=jnp.int32)
    projected = jnp.dot(tokens, wq, preferred_element_type=jnp.float32).reshape(SEQS, Q_LEN, HEADS, HEAD)
    query = (rotate(projected, positions) * (HEAD ** -0.5)).astype(jnp.bfloat16)
    keys = key_cache.reshape(SEQS, KEYS // BLOCK, BLOCK, KV_HEADS, HEAD)
    values = value_cache.reshape(SEQS, KEYS // BLOCK, BLOCK, KV_HEADS, HEAD)
    own_block = (KEYS - Q_LEN) // BLOCK + jnp.arange(QB, dtype=jnp.int32)
    causal = jnp.arange(BLOCK)[None, :] <= jnp.arange(BLOCK)[:, None]

    def one_sequence(items):
        query_seq, keys_seq, values_seq, lists = items
        picked_keys = jnp.take(keys_seq, lists, axis=0).astype(jnp.float32)
        picked_values = jnp.take(values_seq, lists, axis=0).astype(jnp.float32)
        shaped = query_seq.reshape(QB, BLOCK, KV_HEADS, group_size, HEAD).astype(jnp.float32)
        scores = jnp.einsum("bqkgd,bnskd->bkgqns", shaped, picked_keys)
        own = lists == own_block[:, None]
        allowed = jnp.logical_or(jnp.logical_not(own)[:, None, None, None, :, None], causal[None, None, None, :, None, :])
        scores = jnp.where(allowed, scores, -jnp.inf)
        top_score = jnp.max(scores, axis=(4, 5), keepdims=True)
        raised = jnp.exp(scores - top_score)
        weights = (raised / jnp.sum(raised, axis=(4, 5), keepdims=True)).astype(jnp.bfloat16)
        context = jnp.einsum("bkgqns,bnskd->bqkgd", weights.astype(jnp.float32), picked_values)
        return context.astype(jnp.bfloat16).reshape(Q_LEN, HEADS * HEAD)

    contexts = lax.map(one_sequence, (query, keys, values, key_blocks)).reshape(ROWS, HEADS * HEAD)
    group_cols = (HEADS // N_CTX) * HEAD
    total = jnp.zeros((ROWS, D), jnp.float32)
    for index in range(N_CTX):
        share_sum = jnp.dot(contexts[:, index * group_cols:(index + 1) * group_cols], wo[index * group_cols:(index + 1) * group_cols], preferred_element_type=jnp.float32).astype(jnp.bfloat16)
        share_sum = lax.optimization_barrier(share_sum)
        total = total + share_sum.astype(jnp.float32)
    return total.astype(jnp.bfloat16)
```

```python
import functools

import jax
import jax.numpy as jnp
import numpy as np
from jax import lax
from jax.experimental import pallas as pl
from jax.experimental.pallas import tpu as pltpu
from jax.sharding import PartitionSpec as P

HEAD = 128
BLOCK = 128
LANES = 128
AHEAD = 2
HALVES = 2
MESH = pl.DeviceIdType.MESH

rope_base = 1000000.0


def tables(row_count, key_total):
    half_width = HEAD // 2
    exponent = -(np.arange(half_width, dtype=np.float32) * np.float32(2.0)) / np.float32(HEAD)
    frequency = np.power(np.float32(rope_base), exponent, dtype=np.float32)
    positions = (key_total - row_count + np.arange(row_count)).astype(np.float32)
    angles = positions[:, None] * frequency[None, :]
    scale = np.float32(HEAD ** (-0.5))
    cosine = np.cos(angles) * scale
    sine = np.sin(angles) * scale
    return np.concatenate([cosine, cosine], axis=1), np.concatenate([-sine, sine], axis=1)


def low_bit(m):
    return m & -m


def high_bit(m):
    return 1 << (m.bit_length() - 1)


def route(mask, half):
    return low_bit(mask) if half % 2 == 0 else high_bit(mask)


def kernel(
    cfg,
    lists, tokens, wq, wo, kc, vc, cos_in, sin_in,
    out,
    tok, wq_buf, wo_buf, k_buf, v_buf, acc, qc, k_pick, v_pick, bias, ctx_all, ctx_perm, staged, hop, cos_ref, sin_ref,
    tok_sem, own_sem, send_sem, wq_sem, wo_sem, kv_send, kv_sem, ctx_send, ctx_sem,
    move_send, move_sem, keep_sem, hop_send, hop_sem, out_sem,
):
    n_f, n_c, nq, nw = cfg
    chips = n_f // 2
    bits = [1 << i for i in range(chips.bit_length() - 1)]
    levels = len(bits)
    masks = sorted(range(1, chips), key=lambda m: (bin(m).count("1"), m))
    level = {m: bin(m).count("1") for m in masks}
    f = lax.axis_index("fsdp")
    c = lax.axis_index("ctx")
    rows = tok.shape[1]
    depth = tok.shape[2]
    qcols = wq_buf.shape[2]
    qp = qcols // nq
    qh = wq_buf.shape[1] // HALVES
    wo_cols = wo.shape[1]
    wp = wo_buf.shape[2] // nw
    wh = wo_buf.shape[1] // HALVES
    part = wo.shape[0] // chips
    ratio = n_f // n_c
    blk_dev = kc.shape[0]
    kv_cols = k_buf.shape[2]
    group = qcols // kv_cols
    n_blocks = k_buf.shape[0]
    q_blocks = rows // BLOCK
    n_list = lists.shape[2]

    def flip(x):
        bit, total = 1, 0
        while bit < n_f:
            total += lax.rem(lax.div(f, bit) + x // bit, 2) * bit
            bit *= 2
        return total

    def peer(x):
        return (flip(x), c)

    sent = []

    def view(kind, ref, s, h):
        if kind == 0:
            return ref.at[pl.ds(h * qh, qh), pl.ds(s * qp, qp)]
        return ref.at[pl.ds(h * wh, wh), pl.ds(s * wp, wp)]

    shard = (wq, wo_buf.at[0])
    bufs = (wq_buf, wo_buf)
    sems = (wq_sem, wo_sem)
    stream = [(0, s) for s in range(nq)] + [(1, s) for s in range(nw)]

    def send(kind, src, slot, s, h, to):
        copy = pltpu.make_async_remote_copy(
            src_ref=src,
            dst_ref=view(kind, bufs[kind].at[slot], s, h),
            send_sem=send_sem.at[len(sent)],
            recv_sem=sems[kind].at[slot, s, h],
            device_id=peer(to),
            device_id_type=MESH,
        )
        copy.start()
        sent.append(copy)

    def arrived(kind, slot, s, h):
        pltpu.make_async_remote_copy(
            src_ref=view(kind, bufs[kind].at[slot], s, h),
            dst_ref=view(kind, bufs[kind].at[slot], s, h),
            send_sem=send_sem.at[0],
            recv_sem=sems[kind].at[slot, s, h],
            device_id=peer(1),
            device_id_type=MESH,
        ).wait_recv()

    def directs(i):
        if i < len(stream):
            kind, s = stream[i]
            for h in range(HALVES):
                for b in bits:
                    send(kind, view(kind, shard[kind], s, h), 2 * b, s, h, 2 * b)

    def to_partner(kind, s):
        for h in range(HALVES):
            send(kind, view(kind, shard[kind], s, h), 1, s, h, 1)

    def pass_level(i, lev):
        if not 0 <= i < len(stream):
            return
        kind, s = stream[i]
        for h in range(HALVES):
            for m in masks:
                if level[m] != lev:
                    continue
                arrived(kind, 2 * m, s, h)
                block = view(kind, bufs[kind].at[2 * m], s, h)
                for b in bits:
                    if not (m & b) and route(m | b, h) == b:
                        send(kind, block, 2 * (m | b), s, h, 2 * b)
                send(kind, block, 2 * m + 1, s, h, 1)

    def kv_copy(which, d):
        other = lax.rem(c + d, n_c)
        src, dst = ((kc, k_buf), (vc, v_buf))[which]
        return pltpu.make_async_remote_copy(
            src_ref=src.at[:, :, pl.ds(pl.multiple_of(other * kv_cols, LANES), kv_cols)],
            dst_ref=dst.at[pl.ds(c * blk_dev, blk_dev)],
            send_sem=kv_send.at[which, d],
            recv_sem=kv_sem.at[which, d],
            device_id=(f, other),
            device_id_type=MESH,
        )

    core = lax.rem(f, 2)
    chip = lax.div(f, 2)

    def piece(q):
        return wo.at[pl.ds(pl.multiple_of(q * part, part), part), :]

    def hop_copy(q, source):
        return pltpu.make_async_remote_copy(
            src_ref=piece(q),
            dst_ref=hop.at[source],
            send_sem=hop_send.at[q],
            recv_sem=hop_sem.at[source],
            device_id=(q * 2 + core, c),
            device_id_type=MESH,
        )

    def move_dst(i, plane):
        return wo_buf.at[
            0,
            pl.ds(pl.multiple_of(plane * part, part), part),
            pl.ds(pl.multiple_of(i * wo_cols, wo_cols), wo_cols),
        ]

    def owner(p):
        source = p * 2 + core
        return lax.div(source, ratio), lax.div(lax.rem(source, ratio), 2)

    def move(src, p):
        home, i = owner(p)
        return pltpu.make_async_remote_copy(
            src_ref=src,
            dst_ref=move_dst(i, c),
            send_sem=move_send.at[p],
            recv_sem=move_sem.at[i, c],
            device_id=(f, home),
            device_id_type=MESH,
        )

    def keep(src, p):
        _, i = owner(p)
        return pltpu.make_async_copy(src, move_dst(i, c), keep_sem.at[i])

    def forward(src, p):
        home, _ = owner(p)

        @pl.when(home == c)
        def _():
            keep(src, p).start()

        @pl.when(home != c)
        def _():
            move(src, p).start()

    def start_moves():
        forward(piece(chip), chip)

        @pl.loop(1, chips)
        def _(d):
            p = lax.rem(chip + d, chips)
            hop_copy(p, p).wait_recv()
            forward(hop.at[p], p)

    def wait_moves():
        for i in range(ratio // 2):
            keep(piece(chip), lax.div(c * ratio + 2 * i, 2)).wait()

            @pl.loop(1, n_c)
            def _(d):
                plane = lax.rem(c + d, n_c)
                pltpu.make_async_remote_copy(
                    src_ref=move_dst(i, plane),
                    dst_ref=move_dst(i, plane),
                    send_sem=move_send.at[0],
                    recv_sem=move_sem.at[i, plane],
                    device_id=peer(1),
                    device_id_type=MESH,
                ).wait_recv()

    def ctx_view(s, origin):
        return ctx_all.at[origin, :, pl.ds(s * qp, qp)]

    def ctx_copy(s, origin, side, src):
        return pltpu.make_async_remote_copy(
            src_ref=src,
            dst_ref=ctx_view(s, origin),
            send_sem=ctx_send.at[s, origin, side],
            recv_sem=ctx_sem.at[s, origin],
            device_id=(f, c + 1 if side else c - 1),
            device_id_type=MESH,
        )

    def ctx_start(s):
        own = qc.at[:, pl.ds(s * qp, qp)]

        @pl.when(c + 1 < n_c)
        def _():
            ctx_copy(s, c, 1, own).start()

        @pl.when(c > 0)
        def _():
            ctx_copy(s, c, 0, own).start()

        ctx_all[c, :, s * qp:(s + 1) * qp] = qc[:, s * qp:(s + 1) * qp]

    def ctx_pass(s, d):
        below = c - d
        above = c + d

        @pl.when(below >= 0)
        def _():
            ctx_copy(s, below, 0, ctx_view(s, below)).wait_recv()

            @pl.when(c + 1 < n_c)
            def _():
                ctx_copy(s, below, 1, ctx_view(s, below)).start()

        @pl.when(above < n_c)
        def _():
            ctx_copy(s, above, 1, ctx_view(s, above)).wait_recv()

            @pl.when(c > 0)
            def _():
                ctx_copy(s, above, 0, ctx_view(s, above)).start()

    def ctx_drain(s):
        @pl.loop(0, n_c)
        def _(origin):
            @pl.when(jnp.logical_and(origin <= c, c + 1 < n_c))
            def _():
                ctx_copy(s, origin, 1, ctx_view(s, origin)).wait_send()

            @pl.when(jnp.logical_and(origin >= c, c > 0))
            def _():
                ctx_copy(s, origin, 0, ctx_view(s, origin)).wait_send()

    tile = min(256, qp)

    def q_part(j, s):
        for t in range(qp // tile):
            cols = slice(s * qp + t * tile, s * qp + (t + 1) * tile)
            acc[:, cols] += jnp.dot(tok[j], wq_buf[j, :, cols], preferred_element_type=jnp.float32)

    def attend(s):
        first = s * qp // HEAD
        heads = range(first, first + qp // HEAD)
        for h in heads:
            cols = slice(h * HEAD, (h + 1) * HEAD)
            x = acc[:, cols]
            turned = x * cos_ref[...] + pltpu.roll(x, HEAD // 2, 1) * sin_ref[...]
            qc[:, cols] = turned.astype(jnp.bfloat16)

        @pl.loop(0, q_blocks)
        def _(b):
            q_rows = pl.ds(pl.multiple_of(b * BLOCK, BLOCK), BLOCK)
            own_block = n_blocks - q_blocks + b
            later = lax.broadcasted_iota(jnp.int32, (BLOCK, BLOCK), 1) > lax.broadcasted_iota(
                jnp.int32, (BLOCK, BLOCK), 0
            )
            for n in range(n_list):
                entry = lists[0, b, n]
                hide = jnp.where(entry == own_block, -jnp.inf, 0.0)
                bias[:, n * BLOCK:(n + 1) * BLOCK] = jnp.where(later, hide, 0.0)
            for g in sorted({h // group for h in heads}):
                head_cols = slice(g * HEAD, (g + 1) * HEAD)
                for n in range(n_list):
                    entry = lists[0, b, n]
                    k_pick[n * BLOCK:(n + 1) * BLOCK, :] = k_buf[entry, :, head_cols]
                    v_pick[n * BLOCK:(n + 1) * BLOCK, :] = v_buf[entry, :, head_cols]
                for h in heads:
                    if h // group != g:
                        continue
                    cols = slice(h * HEAD, (h + 1) * HEAD)
                    scores = lax.dot_general(
                        qc[q_rows, cols], k_pick[...], (((1,), (1,)), ((), ())),
                        preferred_element_type=jnp.float32,
                    ) + bias[...]
                    top = jnp.max(scores, axis=1, keepdims=True)
                    raised = jnp.exp(scores - top)
                    total = jnp.sum(raised, axis=1, keepdims=True)
                    mixed = jnp.dot(
                        raised.astype(jnp.bfloat16), v_pick[...], preferred_element_type=jnp.float32
                    )
                    qc[q_rows, cols] = (mixed / total).astype(jnp.bfloat16)

    def share(j, s):
        target = flip(j)
        i, offset = divmod(s * wp, wo_cols)
        start = pl.multiple_of((2 * i + lax.rem(target, 2)) * wo_cols + offset, LANES)
        acc[:, pl.ds(start, wp)] += jnp.dot(
            ctx_perm[lax.div(target, 2)], wo_buf[j, :, s * wp:(s + 1) * wp],
            preferred_element_type=jnp.float32,
        )

    def out_copy(s, k):
        i, offset = divmod(s * wp, wo_cols)
        cols = pl.ds((2 * i + k) * wo_cols + offset, wp)
        return pltpu.make_async_copy(staged.at[:, cols], out.at[:, cols], out_sem.at[s, k])

    last_slot = 2 * min(m for m in masks if level[m] == levels)

    def shares(s, start, stop):
        @pl.loop(start, stop)
        def _(j):
            @pl.when(lax.rem(j, 2) == 1)
            def _():
                for h in range(HALVES):
                    arrived(1, j, s, h)

            share(j, s)

    def compute_early(i):
        kind, s = stream[i]
        if kind == 1 and levels > 1:
            shares(s, 0, 4)
            if levels == 2:
                shares(s, 4, last_slot)

    def compute(i):
        kind, s = stream[i]
        if kind == 0:
            @pl.loop(2, n_f)
            def _(j):
                @pl.when(lax.rem(j, 2) == 1)
                def _():
                    for h in range(HALVES):
                        arrived(0, j, s, h)

                q_part(j, s)

            attend(s)
            ctx_start(s)
            return
        shares(s, (last_slot if levels == 2 else 4) if levels > 1 else 0, n_f)
        for k in range(2):
            p, offset = divmod(s * wp, wo_cols)
            cols = pl.ds((2 * p + k) * wo_cols + offset, wp)
            staged[:, cols] = acc[:, cols].astype(jnp.bfloat16)
            out_copy(s, k).start()

    def tok_copy(j):
        start = pl.multiple_of(flip(j) * depth, LANES)
        return pltpu.make_async_copy(tokens.at[:, pl.ds(start, depth)], tok.at[j], tok_sem.at[j])

    mine = pl.ds(pl.multiple_of(c * kv_cols, LANES), kv_cols)
    locals_in = [
        pltpu.make_async_copy(wq, wq_buf.at[0], own_sem.at[0]),
        pltpu.make_async_copy(kc.at[:, :, mine], k_buf.at[pl.ds(c * blk_dev, blk_dev)], own_sem.at[1]),
        pltpu.make_async_copy(vc.at[:, :, mine], v_buf.at[pl.ds(c * blk_dev, blk_dev)], own_sem.at[2]),
        pltpu.make_async_copy(cos_in, cos_ref, own_sem.at[3]),
        pltpu.make_async_copy(sin_in, sin_ref, own_sem.at[4]),
    ]

    barrier = pltpu.get_barrier_semaphore()
    signalled = 0
    for x in [1] + [2 * m for m in masks]:
        pl.semaphore_signal(barrier, inc=1, device_id=peer(x), device_id_type=MESH)
        signalled += 1
    for d in range(1, n_c):
        pl.semaphore_signal(barrier, inc=1, device_id=(f, lax.rem(c + d, n_c)), device_id_type=MESH)
        signalled += 1
    for copy in locals_in:
        copy.start()
    for j in range(n_f):
        tok_copy(j).start()
    acc[...] = jnp.zeros_like(acc)
    pl.semaphore_wait(barrier, signalled)

    @pl.loop(1, chips)
    def _(d):
        hop_copy(lax.rem(chip + d, chips), chip).start()

    kv_sent = []
    for d in range(1, n_c):
        for which in range(2):
            copy = kv_copy(which, d)
            copy.start()
            kv_sent.append(copy)
    for i in range(AHEAD):
        directs(i)
    for s in range(nq):
        to_partner(0, s)

    locals_in[0].wait()
    for j in range(n_f):
        tok_copy(j).wait()
    start_moves()
    for s in range(nq):
        for h in range(HALVES):
            arrived(0, 1, s, h)

        @pl.loop(0, 2)
        def _(j):
            q_part(j, s)

    for copy in locals_in[1:]:
        copy.wait()

    lag = levels - 1
    total = len(stream)
    done = {}
    for step in range(total + lag):
        pass_level(step, 1)
        if step + AHEAD < total:
            directs(step + AHEAD)
        i = step - lag
        for lev in range(2, levels):
            pass_level(step - lev + 1, lev)
        for s in range(nq):
            if s in done and done[s] < n_c:
                if i == nq:
                    while done[s] < n_c:
                        ctx_pass(s, done[s])
                        done[s] += 1
                else:
                    ctx_pass(s, done[s])
                    done[s] += 1
        if i == nq:
            for q in range(chips):
                for plane in range(n_c):
                    ctx_perm[q, :, plane * part:(plane + 1) * part] = ctx_all[
                        plane, :, q * part:(q + 1) * part
                    ]
        if i >= 0:
            if levels > 1:
                compute_early(i)
                pass_level(i, levels)
            if i == 0:
                for copy in kv_sent:
                    copy.wait_recv()
            compute(i)
            if stream[i][0] == 0:
                done[stream[i][1]] = 1
            if i == nq - 1:
                acc[...] = jnp.zeros_like(acc)
                ctx_pass(nq - 1, 1)
                done[nq - 1] = 2
        if step + 1 + AHEAD == max(nq, AHEAD + 1):
            wait_moves()
            for s in range(nw):
                to_partner(1, s)

    assert len(sent) == send_sem.shape[0]
    for copy in sent + kv_sent:
        copy.wait_send()
    for s in range(nq):
        ctx_drain(s)

    @pl.loop(0, chips)
    def _(q):
        @pl.when(q != chip)
        def _():
            hop_copy(q, chip).wait_send()

        home, _ = owner(q)

        @pl.when(home != c)
        def _():
            move(piece(chip), q).wait_send()

    for s in range(nw):
        for k in range(2):
            out_copy(s, k).wait()


def body(n_f, n_c, tokens, wq, wo, key_cache, value_cache, key_blocks):
    rows, width = tokens.shape
    depth = width // n_f
    qcols = wq.shape[1]
    cache = key_cache.shape[0]
    blk_dev = cache // BLOCK
    kv_cols = key_cache.shape[1] // n_c
    n_list = key_blocks.shape[2]
    cosine, sine = tables(rows, cache * n_c)
    nq = max(1, min(4, qcols // HEAD))
    ratio = n_f // n_c
    chips = n_f // 2
    part = wo.shape[0] // chips
    moved = (part * n_c, wo.shape[1] * ratio // 2)
    nw = max(1, min(4, moved[1] // LANES))
    any_spec = pl.BlockSpec(memory_space=pl.ANY)
    bf16 = jnp.bfloat16
    f32 = jnp.float32
    dma = pltpu.SemaphoreType.DMA
    return pl.pallas_call(
        functools.partial(kernel, (n_f, n_c, nq, nw)),
        out_shape=jax.ShapeDtypeStruct((rows, width // n_c), bf16),
        in_specs=[pl.BlockSpec(memory_space=pltpu.SMEM)] + [any_spec] * 7,
        out_specs=any_spec,
        scratch_shapes=[
            pltpu.VMEM((n_f, rows, depth), bf16),
            pltpu.VMEM((n_f,) + wq.shape, bf16),
            pltpu.VMEM((n_f,) + moved, bf16),
            pltpu.VMEM((blk_dev * n_c, BLOCK, kv_cols), bf16),
            pltpu.VMEM((blk_dev * n_c, BLOCK, kv_cols), bf16),
            pltpu.VMEM((rows, max(qcols, width // n_c)), f32),
            pltpu.VMEM((rows, qcols), bf16),
            pltpu.VMEM((n_list * BLOCK, HEAD), bf16),
            pltpu.VMEM((n_list * BLOCK, HEAD), bf16),
            pltpu.VMEM((BLOCK, n_list * BLOCK), f32),
            pltpu.VMEM((n_c, rows, qcols), bf16),
            pltpu.VMEM((chips, rows, n_c * part), bf16),
            pltpu.VMEM((rows, width // n_c), bf16),
            pltpu.VMEM((chips, part, wo.shape[1]), bf16),
            pltpu.VMEM((rows, HEAD), f32),
            pltpu.VMEM((rows, HEAD), f32),
            dma((n_f,)),
            dma((5,)),
            dma(((nq + nw) * HALVES * (n_f - 1),)),
            dma((n_f, nq, HALVES)),
            dma((n_f, nw, HALVES)),
            dma((2, n_c)),
            dma((2, n_c)),
            dma((nq, n_c, 2)),
            dma((nq, n_c)),
            dma((chips,)),
            dma((ratio // 2, n_c)),
            dma((ratio // 2,)),
            dma((chips,)),
            dma((chips,)),
            dma((nw, 2)),
        ],
        compiler_params=pltpu.CompilerParams(
            collective_id=0, has_side_effects=True, vmem_limit_bytes=67043328
        ),
    )(
        key_blocks,
        tokens,
        wq,
        wo,
        key_cache.reshape(blk_dev, BLOCK, key_cache.shape[1]),
        value_cache.reshape(blk_dev, BLOCK, value_cache.shape[1]),
        jnp.asarray(cosine, jnp.float32),
        jnp.asarray(sine, jnp.float32),
    )


def solution(mesh):
    in_specs = (
        P("fsdp", None),
        P("fsdp", "ctx"),
        P("ctx", "fsdp"),
        P(("fsdp", "ctx"), None),
        P(("fsdp", "ctx"), None),
        P("fsdp", None, None),
    )
    step = functools.partial(body, mesh.shape["fsdp"], mesh.shape["ctx"])
    return jax.shard_map(
        step, mesh=mesh, in_specs=in_specs, out_specs=P("fsdp", "ctx"), check_vma=False
    )
```

```python
import functools

import jax
import jax.numpy as jnp
import numpy as np
from jax import lax
from jax.experimental import pallas as pl
from jax.experimental.pallas import tpu as pltpu
from jax.sharding import PartitionSpec as P

HEAD = 128
BLOCK = 128
LANES = 128
AHEAD = 2
HALVES = 2
MESH = pl.DeviceIdType.MESH

rope_base = 1000000.0


def tables(row_count, key_total):
    half_width = HEAD // 2
    exponent = -(np.arange(half_width, dtype=np.float32) * np.float32(2.0)) / np.float32(HEAD)
    frequency = np.power(np.float32(rope_base), exponent, dtype=np.float32)
    positions = (key_total - row_count + np.arange(row_count)).astype(np.float32)
    angles = positions[:, None] * frequency[None, :]
    scale = np.float32(HEAD ** (-0.5))
    cosine = np.cos(angles) * scale
    sine = np.sin(angles) * scale
    return np.concatenate([cosine, cosine], axis=1), np.concatenate([-sine, sine], axis=1)


def low_bit(m):
    return m & -m


def high_bit(m):
    return 1 << (m.bit_length() - 1)


def route(mask, half):
    return low_bit(mask) if half % 2 == 0 else high_bit(mask)


def kernel(
    cfg,
    lists, tokens, wq, wo, kc, vc, cos_in, sin_in,
    out,
    tok, wq_buf, wo_buf, k_buf, v_buf, acc, qc, k_pick, v_pick, bias, ctx_all, ctx_perm, staged, hop, cos_ref, sin_ref,
    rs_buf, rs_sum, rs_recv,
    tok_sem, own_sem, send_sem, wq_sem, wo_sem, kv_send, kv_sem, ctx_send, ctx_sem,
    move_send, move_sem, keep_sem, hop_send, hop_sem, out_sem, rs_sem, give_send, give_sem,
):
    n_f, n_c, nq, nw, rs_cols = cfg
    chips = n_f // 2
    bits = [1 << i for i in range(chips.bit_length() - 1)]
    levels = len(bits)
    masks = sorted(range(1, chips), key=lambda m: (bin(m).count("1"), m))
    level = {m: bin(m).count("1") for m in masks}
    f = lax.axis_index("fsdp")
    c = lax.axis_index("ctx")
    rows = tok.shape[1]
    depth = tok.shape[2]
    qcols = wq_buf.shape[2]
    qp = qcols // nq
    qh = wq_buf.shape[1] // HALVES
    wo_cols = wo.shape[1]
    t_cols = wo_cols - rs_cols
    rh = wo.shape[0] // HALVES
    wp = wo_buf.shape[2] // nw
    wh = wo_buf.shape[1] // HALVES
    part = wo.shape[0] // chips
    ratio = n_f // n_c
    blk_dev = kc.shape[0]
    kv_cols = k_buf.shape[2]
    group = qcols // kv_cols
    n_blocks = k_buf.shape[0]
    q_blocks = rows // BLOCK
    n_list = lists.shape[2]

    def flip(x):
        bit, total = 1, 0
        while bit < n_f:
            total += lax.rem(lax.div(f, bit) + x // bit, 2) * bit
            bit *= 2
        return total

    def peer(x):
        return (flip(x), c)

    sent = []

    def view(kind, ref, s, h):
        if kind == 0:
            return ref.at[pl.ds(h * qh, qh), pl.ds(s * qp, qp)]
        if kind == 2:
            return ref.at[pl.ds(h * rh, rh), pl.ds(0, rs_cols)]
        return ref.at[pl.ds(h * wh, wh), pl.ds(s * wp, wp)]

    shard = (wq, wo_buf.at[0], wo)
    bufs = (wq_buf, wo_buf, rs_buf)
    sems = (wq_sem, wo_sem, rs_sem)
    stream = [(0, s) for s in range(nq)] + ([(2, 0)] if rs_cols else []) + [(1, s) for s in range(nw)]
    first_wo = stream.index((1, 0))

    def send(kind, src, slot, s, h, to):
        copy = pltpu.make_async_remote_copy(
            src_ref=src,
            dst_ref=view(kind, bufs[kind].at[slot], s, h),
            send_sem=send_sem.at[len(sent)],
            recv_sem=sems[kind].at[slot, s, h],
            device_id=peer(to),
            device_id_type=MESH,
        )
        copy.start()
        sent.append(copy)

    def arrived(kind, slot, s, h):
        pltpu.make_async_remote_copy(
            src_ref=view(kind, bufs[kind].at[slot], s, h),
            dst_ref=view(kind, bufs[kind].at[slot], s, h),
            send_sem=send_sem.at[0],
            recv_sem=sems[kind].at[slot, s, h],
            device_id=peer(1),
            device_id_type=MESH,
        ).wait_recv()

    def directs(i):
        if i < len(stream):
            kind, s = stream[i]
            for h in range(HALVES):
                for b in bits:
                    send(kind, view(kind, shard[kind], s, h), 2 * b, s, h, 2 * b)

    def to_partner(kind, s):
        for h in range(HALVES):
            send(kind, view(kind, shard[kind], s, h), 1, s, h, 1)

    def pass_level(i, lev):
        if not 0 <= i < len(stream):
            return
        kind, s = stream[i]
        for h in range(HALVES):
            for m in masks:
                if level[m] != lev:
                    continue
                arrived(kind, 2 * m, s, h)
                block = view(kind, bufs[kind].at[2 * m], s, h)
                for b in bits:
                    if not (m & b) and route(m | b, h) == b:
                        send(kind, block, 2 * (m | b), s, h, 2 * b)
                send(kind, block, 2 * m + 1, s, h, 1)

    def kv_copy(which, d):
        other = lax.rem(c + d, n_c)
        src, dst = ((kc, k_buf), (vc, v_buf))[which]
        return pltpu.make_async_remote_copy(
            src_ref=src.at[:, :, pl.ds(pl.multiple_of(other * kv_cols, LANES), kv_cols)],
            dst_ref=dst.at[pl.ds(c * blk_dev, blk_dev)],
            send_sem=kv_send.at[which, d],
            recv_sem=kv_sem.at[which, d],
            device_id=(f, other),
            device_id_type=MESH,
        )

    core = lax.rem(f, 2)
    chip = lax.div(f, 2)

    def piece(q):
        return wo.at[pl.ds(pl.multiple_of(q * part, part), part), pl.ds(rs_cols, t_cols)]

    def hop_copy(q, source):
        return pltpu.make_async_remote_copy(
            src_ref=piece(q),
            dst_ref=hop.at[source],
            send_sem=hop_send.at[q],
            recv_sem=hop_sem.at[source],
            device_id=(q * 2 + core, c),
            device_id_type=MESH,
        )

    def move_dst(i, plane):
        return wo_buf.at[
            0,
            pl.ds(pl.multiple_of(plane * part, part), part),
            pl.ds(pl.multiple_of(i * t_cols, t_cols), t_cols),
        ]

    def owner(p):
        source = p * 2 + core
        return lax.div(source, ratio), lax.div(lax.rem(source, ratio), 2)

    def move(src, p):
        home, i = owner(p)
        return pltpu.make_async_remote_copy(
            src_ref=src,
            dst_ref=move_dst(i, c),
            send_sem=move_send.at[p],
            recv_sem=move_sem.at[i, c],
            device_id=(f, home),
            device_id_type=MESH,
        )

    def keep(src, p):
        _, i = owner(p)
        return pltpu.make_async_copy(src, move_dst(i, c), keep_sem.at[i])

    def forward(src, p):
        home, _ = owner(p)

        @pl.when(home == c)
        def _():
            keep(src, p).start()

        @pl.when(home != c)
        def _():
            move(src, p).start()

    def start_moves():
        forward(piece(chip), chip)

        @pl.loop(1, chips)
        def _(d):
            p = lax.rem(chip + d, chips)
            hop_copy(p, p).wait_recv()
            forward(hop.at[p], p)

    def wait_moves():
        for i in range(ratio // 2):
            keep(piece(chip), lax.div(c * ratio + 2 * i, 2)).wait()

            @pl.loop(1, n_c)
            def _(d):
                plane = lax.rem(c + d, n_c)
                pltpu.make_async_remote_copy(
                    src_ref=move_dst(i, plane),
                    dst_ref=move_dst(i, plane),
                    send_sem=move_send.at[0],
                    recv_sem=move_sem.at[i, plane],
                    device_id=peer(1),
                    device_id_type=MESH,
                ).wait_recv()

    def ctx_view(s, origin):
        return ctx_all.at[origin, :, pl.ds(s * qp, qp)]

    def ctx_copy(s, origin, side, src):
        return pltpu.make_async_remote_copy(
            src_ref=src,
            dst_ref=ctx_view(s, origin),
            send_sem=ctx_send.at[s, origin, side],
            recv_sem=ctx_sem.at[s, origin],
            device_id=(f, c + 1 if side else c - 1),
            device_id_type=MESH,
        )

    def ctx_start(s):
        own = qc.at[:, pl.ds(s * qp, qp)]

        @pl.when(c + 1 < n_c)
        def _():
            ctx_copy(s, c, 1, own).start()

        @pl.when(c > 0)
        def _():
            ctx_copy(s, c, 0, own).start()

        ctx_all[c, :, s * qp:(s + 1) * qp] = qc[:, s * qp:(s + 1) * qp]

    def ctx_pass(s, d):
        below = c - d
        above = c + d

        @pl.when(below >= 0)
        def _():
            ctx_copy(s, below, 0, ctx_view(s, below)).wait_recv()

            @pl.when(c + 1 < n_c)
            def _():
                ctx_copy(s, below, 1, ctx_view(s, below)).start()

        @pl.when(above < n_c)
        def _():
            ctx_copy(s, above, 1, ctx_view(s, above)).wait_recv()

            @pl.when(c > 0)
            def _():
                ctx_copy(s, above, 0, ctx_view(s, above)).start()

    def ctx_drain(s):
        @pl.loop(0, n_c)
        def _(origin):
            @pl.when(jnp.logical_and(origin <= c, c + 1 < n_c))
            def _():
                ctx_copy(s, origin, 1, ctx_view(s, origin)).wait_send()

            @pl.when(jnp.logical_and(origin >= c, c > 0))
            def _():
                ctx_copy(s, origin, 0, ctx_view(s, origin)).wait_send()

    tile = min(256, qp)

    def q_part(j, s):
        for t in range(qp // tile):
            cols = slice(s * qp + t * tile, s * qp + (t + 1) * tile)
            acc[:, cols] += jnp.dot(tok[j], wq_buf[j, :, cols], preferred_element_type=jnp.float32)

    def attend(s):
        first = s * qp // HEAD
        heads = range(first, first + qp // HEAD)
        for h in heads:
            cols = slice(h * HEAD, (h + 1) * HEAD)
            x = acc[:, cols]
            turned = x * cos_ref[...] + pltpu.roll(x, HEAD // 2, 1) * sin_ref[...]
            qc[:, cols] = turned.astype(jnp.bfloat16)

        @pl.loop(0, q_blocks)
        def _(b):
            q_rows = pl.ds(pl.multiple_of(b * BLOCK, BLOCK), BLOCK)
            own_block = n_blocks - q_blocks + b
            later = lax.broadcasted_iota(jnp.int32, (BLOCK, BLOCK), 1) > lax.broadcasted_iota(
                jnp.int32, (BLOCK, BLOCK), 0
            )
            for n in range(n_list):
                entry = lists[0, b, n]
                hide = jnp.where(entry == own_block, -jnp.inf, 0.0)
                bias[:, n * BLOCK:(n + 1) * BLOCK] = jnp.where(later, hide, 0.0)
            for g in sorted({h // group for h in heads}):
                head_cols = slice(g * HEAD, (g + 1) * HEAD)
                for n in range(n_list):
                    entry = lists[0, b, n]
                    k_pick[n * BLOCK:(n + 1) * BLOCK, :] = k_buf[entry, :, head_cols]
                    v_pick[n * BLOCK:(n + 1) * BLOCK, :] = v_buf[entry, :, head_cols]
                for h in heads:
                    if h // group != g:
                        continue
                    cols = slice(h * HEAD, (h + 1) * HEAD)
                    scores = lax.dot_general(
                        qc[q_rows, cols], k_pick[...], (((1,), (1,)), ((), ())),
                        preferred_element_type=jnp.float32,
                    ) + bias[...]
                    top = jnp.max(scores, axis=1, keepdims=True)
                    raised = jnp.exp(scores - top)
                    total = jnp.sum(raised, axis=1, keepdims=True)
                    mixed = jnp.dot(
                        raised.astype(jnp.bfloat16), v_pick[...], preferred_element_type=jnp.float32
                    )
                    qc[q_rows, cols] = (mixed / total).astype(jnp.bfloat16)

    def share(j, s):
        target = flip(j)
        i, offset = divmod(s * wp, t_cols)
        start = pl.multiple_of((2 * i + lax.rem(target, 2)) * wo_cols + rs_cols + offset, LANES)
        acc[:, pl.ds(start, wp)] += jnp.dot(
            ctx_perm[lax.div(target, 2)], wo_buf[j, :, s * wp:(s + 1) * wp],
            preferred_element_type=jnp.float32,
        )

    def out_cols(s, k):
        if s == nw:
            return pl.ds(k * wo_cols, rs_cols)
        i, offset = divmod(s * wp, t_cols)
        return pl.ds((2 * i + k) * wo_cols + rs_cols + offset, wp)

    def out_copy(s, k):
        cols = out_cols(s, k)
        return pltpu.make_async_copy(staged.at[:, cols], out.at[:, cols], out_sem.at[s, k])

    def gift(home, k):
        return tok.at[home, :, pl.ds(k * rs_cols, rs_cols)]

    def give(home, k, side):
        slot = jnp.where(home == c + 2 * side - 1, n_c * (1 - side) + home * side, home)
        return pltpu.make_async_remote_copy(
            src_ref=gift(home, k),
            dst_ref=rs_recv.at[slot, k],
            send_sem=give_send.at[home, k],
            recv_sem=give_sem.at[slot, k],
            device_id=(f, c + 2 * side - 1),
            device_id_type=MESH,
        )

    def got(slot, k):
        pltpu.make_async_remote_copy(
            src_ref=rs_recv.at[slot, k],
            dst_ref=rs_recv.at[slot, k],
            send_sem=give_send.at[0, k],
            recv_sem=give_sem.at[slot, k],
            device_id=peer(1),
            device_id_type=MESH,
        ).wait_recv()

    def rs_start():
        locals_in[5].wait()

        @pl.loop(0, n_f)
        def _(j):
            @pl.when(lax.rem(j, 2) == 1)
            def _():
                for h in range(HALVES):
                    arrived(2, j, 0, h)

            target = flip(j)
            cols = pl.ds(pl.multiple_of(lax.rem(target, 2) * rs_cols, LANES), rs_cols)
            tok[lax.div(target, 2), :, cols] = jnp.dot(
                qc[...], rs_buf[j], preferred_element_type=jnp.float32
            ).astype(jnp.bfloat16)

        @pl.when(c == 0)
        def _():
            for home in range(n_c - 1, 0, -1):
                for k in range(2):
                    give(home, k, 1).start()

        @pl.when(c == n_c - 1)
        def _():
            for home in range(n_c - 1):
                for k in range(2):
                    give(home, k, 0).start()

    def rs_pass(e, k):
        def add(home, side):
            got(home, k)
            cols = slice(k * rs_cols, (k + 1) * rs_cols)
            tok[home, :, cols] = (
                tok[home, :, cols].astype(jnp.float32) + rs_recv[home, k].astype(jnp.float32)
            ).astype(jnp.bfloat16)
            give(home, k, side).start()

        @pl.when(jnp.logical_and(c > 0, c + e < n_c))
        def _():
            add(c + e, 1)

        @pl.when(jnp.logical_and(c < n_c - 1, c - e >= 0))
        def _():
            add(c - e, 0)

    def take():
        for k in range(2):
            cols = slice(k * rs_cols, (k + 1) * rs_cols)
            rs_sum[...] = tok[c, :, cols].astype(jnp.float32)

            @pl.when(c > 0)
            def _():
                got(c, k)
                rs_sum[...] += rs_recv[c, k].astype(jnp.float32)

            @pl.when(c < n_c - 1)
            def _():
                got(n_c, k)
                rs_sum[...] += rs_recv[n_c, k].astype(jnp.float32)

            staged[:, out_cols(nw, k)] = rs_sum[...].astype(jnp.bfloat16)
            out_copy(nw, k).start()

    last_slot = 2 * min(m for m in masks if level[m] == levels)

    def shares(s, start, stop):
        @pl.loop(start, stop)
        def _(j):
            @pl.when(lax.rem(j, 2) == 1)
            def _():
                for h in range(HALVES):
                    arrived(1, j, s, h)

            share(j, s)

    def compute_early(i):
        kind, s = stream[i]
        if kind == 1 and levels > 1:
            shares(s, 0, 4)
            if levels == 2:
                shares(s, 4, last_slot)

    def compute(i):
        kind, s = stream[i]
        if kind == 0:
            @pl.loop(2, n_f)
            def _(j):
                @pl.when(lax.rem(j, 2) == 1)
                def _():
                    for h in range(HALVES):
                        arrived(0, j, s, h)

                q_part(j, s)

            attend(s)
            ctx_start(s)
            return
        shares(s, (last_slot if levels == 2 else 4) if levels > 1 else 0, n_f)
        for k in range(2):
            cols = out_cols(s, k)
            staged[:, cols] = acc[:, cols].astype(jnp.bfloat16)
            out_copy(s, k).start()

    def tok_copy(j):
        start = pl.multiple_of(flip(j) * depth, LANES)
        return pltpu.make_async_copy(tokens.at[:, pl.ds(start, depth)], tok.at[j], tok_sem.at[j])

    mine = pl.ds(pl.multiple_of(c * kv_cols, LANES), kv_cols)
    locals_in = [
        pltpu.make_async_copy(wq, wq_buf.at[0], own_sem.at[0]),
        pltpu.make_async_copy(kc.at[:, :, mine], k_buf.at[pl.ds(c * blk_dev, blk_dev)], own_sem.at[1]),
        pltpu.make_async_copy(vc.at[:, :, mine], v_buf.at[pl.ds(c * blk_dev, blk_dev)], own_sem.at[2]),
        pltpu.make_async_copy(cos_in, cos_ref, own_sem.at[3]),
        pltpu.make_async_copy(sin_in, sin_ref, own_sem.at[4]),
    ]
    if rs_cols:
        locals_in.append(pltpu.make_async_copy(wo.at[:, pl.ds(0, rs_cols)], rs_buf.at[0], own_sem.at[5]))

    barrier = pltpu.get_barrier_semaphore()
    signalled = 0
    for x in [1] + [2 * m for m in masks]:
        pl.semaphore_signal(barrier, inc=1, device_id=peer(x), device_id_type=MESH)
        signalled += 1
    for d in range(1, n_c):
        pl.semaphore_signal(barrier, inc=1, device_id=(f, lax.rem(c + d, n_c)), device_id_type=MESH)
        signalled += 1
    for copy in locals_in:
        copy.start()
    for j in range(n_f):
        tok_copy(j).start()
    acc[...] = jnp.zeros_like(acc)
    pl.semaphore_wait(barrier, signalled)

    @pl.loop(1, chips)
    def _(d):
        hop_copy(lax.rem(chip + d, chips), chip).start()

    kv_sent = []
    for d in range(1, n_c):
        for which in range(2):
            copy = kv_copy(which, d)
            copy.start()
            kv_sent.append(copy)
    for i in range(AHEAD):
        directs(i)
    for s in range(nq):
        to_partner(0, s)
    if rs_cols:
        to_partner(2, 0)

    locals_in[0].wait()
    for j in range(n_f):
        tok_copy(j).wait()
    start_moves()
    for s in range(nq):
        for h in range(HALVES):
            arrived(0, 1, s, h)

        @pl.loop(0, 2)
        def _(j):
            q_part(j, s)

    for copy in locals_in[1:5]:
        copy.wait()

    lag = levels - 1
    total = len(stream)
    done = {}
    queued = AHEAD

    def ctx_next(s):
        if done[s] < n_c:
            ctx_pass(s, done[s])
            done[s] += 1

    for step in range(total + lag):
        pass_level(step, 1)
        i = step - lag
        while queued < total and queued <= step + AHEAD and not (rs_cols and step == nq - 1 and queued > nq):
            directs(queued)
            queued += 1
        for lev in range(2, levels):
            pass_level(step - lev + 1, lev)
        for s in range(nq):
            if s in done and not (rs_cols and s == nq - 1):
                ctx_next(s)
        if rs_cols and step == nq + 1:
            for k in range(2):
                for e in range(n_c - 2, 1, -1):
                    rs_pass(e, k)
                ctx_next(nq - 1)
        if i == first_wo:
            for s in range(nq):
                while done[s] < n_c:
                    ctx_next(s)
            for q in range(chips):
                for plane in range(n_c):
                    ctx_perm[q, :, plane * part:(plane + 1) * part] = ctx_all[
                        plane, :, q * part:(q + 1) * part
                    ]
        if i >= 0 and stream[i][0] != 2:
            if levels > 1:
                compute_early(i)
                if rs_cols and step == total + lag - 1:
                    take()
                pass_level(i, levels)
            if i == 0:
                for copy in kv_sent:
                    copy.wait_recv()
            compute(i)
            if stream[i][0] == 0:
                done[stream[i][1]] = 1
            if i == nq - 1:
                if rs_cols:
                    pass_level(nq, 2)
                    rs_start()
                acc[...] = jnp.zeros_like(acc)
                ctx_next(nq - 1)
            if rs_cols and i == first_wo:
                for k in range(2):
                    rs_pass(1, k)
        if step + 1 + AHEAD == max(first_wo, AHEAD + 1):
            wait_moves()
            for s in range(nw):
                to_partner(1, s)

    assert len(sent) == send_sem.shape[0]
    for copy in sent + kv_sent:
        copy.wait_send()
    for s in range(nq):
        ctx_drain(s)

    @pl.loop(0, chips)
    def _(q):
        @pl.when(q != chip)
        def _():
            hop_copy(q, chip).wait_send()

        home, _ = owner(q)

        @pl.when(home != c)
        def _():
            move(piece(chip), q).wait_send()

    if rs_cols:
        for k in range(2):
            @pl.loop(0, n_c)
            def _(home):
                @pl.when(home != c)
                def _():
                    give(home, k, jnp.where(home > c, 1, 0)).wait_send()
    for s in range(nw + (1 if rs_cols else 0)):
        for k in range(2):
            out_copy(s, k).wait()


def body(n_f, n_c, tokens, wq, wo, key_cache, value_cache, key_blocks):
    rows, width = tokens.shape
    depth = width // n_f
    qcols = wq.shape[1]
    cache = key_cache.shape[0]
    blk_dev = cache // BLOCK
    kv_cols = key_cache.shape[1] // n_c
    n_list = key_blocks.shape[2]
    cosine, sine = tables(rows, cache * n_c)
    nq = max(1, min(4, qcols // HEAD))
    ratio = n_f // n_c
    chips = n_f // 2
    part = wo.shape[0] // chips
    rs_cols = wo.shape[1] // 4 if ratio == 2 and n_f == chips * 2 == n_c * 2 and chips.bit_length() == 3 and wo.shape[1] % (4 * LANES) == 0 else 0
    t_cols = wo.shape[1] - rs_cols
    moved = (part * n_c, t_cols * ratio // 2)
    nw = moved[1] // rs_cols if rs_cols else max(1, min(4, moved[1] // LANES))
    rs_shape = (wo.shape[0], rs_cols) if rs_cols else (16, LANES)
    share_shape = (n_c + 1, 2, rows, rs_cols) if rs_cols else (1, 1, 16, LANES)
    any_spec = pl.BlockSpec(memory_space=pl.ANY)
    bf16 = jnp.bfloat16
    f32 = jnp.float32
    dma = pltpu.SemaphoreType.DMA
    return pl.pallas_call(
        functools.partial(kernel, (n_f, n_c, nq, nw, rs_cols)),
        out_shape=jax.ShapeDtypeStruct((rows, width // n_c), bf16),
        in_specs=[pl.BlockSpec(memory_space=pltpu.SMEM)] + [any_spec] * 7,
        out_specs=any_spec,
        scratch_shapes=[
            pltpu.VMEM((n_f, rows, depth), bf16),
            pltpu.VMEM((n_f,) + wq.shape, bf16),
            pltpu.VMEM((n_f,) + moved, bf16),
            pltpu.VMEM((blk_dev * n_c, BLOCK, kv_cols), bf16),
            pltpu.VMEM((blk_dev * n_c, BLOCK, kv_cols), bf16),
            pltpu.VMEM((rows, max(qcols, width // n_c)), f32),
            pltpu.VMEM((rows, qcols), bf16),
            pltpu.VMEM((n_list * BLOCK, HEAD), bf16),
            pltpu.VMEM((n_list * BLOCK, HEAD), bf16),
            pltpu.VMEM((BLOCK, n_list * BLOCK), f32),
            pltpu.VMEM((n_c, rows, qcols), bf16),
            pltpu.VMEM((chips, rows, n_c * part), bf16),
            pltpu.VMEM((rows, width // n_c), bf16),
            pltpu.VMEM((chips, part, t_cols), bf16),
            pltpu.VMEM((rows, HEAD), f32),
            pltpu.VMEM((rows, HEAD), f32),
            pltpu.VMEM((n_f if rs_cols else 1,) + rs_shape, bf16),
            pltpu.VMEM(share_shape[2:], f32),
            pltpu.VMEM(share_shape, bf16),
            dma((n_f,)),
            dma((6,)),
            dma(((nq + nw + (1 if rs_cols else 0)) * HALVES * (n_f - 1),)),
            dma((n_f, nq, HALVES)),
            dma((n_f, nw, HALVES)),
            dma((2, n_c)),
            dma((2, n_c)),
            dma((nq, n_c, 2)),
            dma((nq, n_c)),
            dma((chips,)),
            dma((ratio // 2, n_c)),
            dma((ratio // 2,)),
            dma((chips,)),
            dma((chips,)),
            dma((nw + 1, 2)),
            dma((n_f, 1, HALVES)),
            dma((n_c, 2)),
            dma((n_c + 1, 2)),
        ],
        compiler_params=pltpu.CompilerParams(
            collective_id=0, has_side_effects=True, vmem_limit_bytes=67043328
        ),
    )(
        key_blocks,
        tokens,
        wq,
        wo,
        key_cache.reshape(blk_dev, BLOCK, key_cache.shape[1]),
        value_cache.reshape(blk_dev, BLOCK, value_cache.shape[1]),
        jnp.asarray(cosine, jnp.float32),
        jnp.asarray(sine, jnp.float32),
    )


def solution(mesh):
    in_specs = (
        P("fsdp", None),
        P("fsdp", "ctx"),
        P("ctx", "fsdp"),
        P(("fsdp", "ctx"), None),
        P(("fsdp", "ctx"), None),
        P("fsdp", None, None),
    )
    step = functools.partial(body, mesh.shape["fsdp"], mesh.shape["ctx"])
    return jax.shard_map(
        step, mesh=mesh, in_specs=in_specs, out_specs=P("fsdp", "ctx"), check_vma=False
    )
```

```python
import functools

import jax
import jax.numpy as jnp
import numpy as np
from jax import lax
from jax.experimental import pallas as pl
from jax.experimental.pallas import tpu as pltpu
from jax.sharding import PartitionSpec as P

HEAD = 128
BLOCK = 128
LANES = 128
AHEAD = 2
HALVES = 2
MESH = pl.DeviceIdType.MESH

rope_base = 1000000.0


def tables(row_count, key_total):
    half_width = HEAD // 2
    exponent = -(np.arange(half_width, dtype=np.float32) * np.float32(2.0)) / np.float32(HEAD)
    frequency = np.power(np.float32(rope_base), exponent, dtype=np.float32)
    positions = (key_total - row_count + np.arange(row_count)).astype(np.float32)
    angles = positions[:, None] * frequency[None, :]
    scale = np.float32(HEAD ** (-0.5))
    cosine = np.cos(angles) * scale
    sine = np.sin(angles) * scale
    return np.concatenate([cosine, cosine], axis=1), np.concatenate([-sine, sine], axis=1)


def low_bit(m):
    return m & -m


def high_bit(m):
    return 1 << (m.bit_length() - 1)


def route(mask, half):
    return low_bit(mask) if half % 2 == 0 else high_bit(mask)


def kernel(
    cfg,
    lists, tokens, wq, wo, kc, vc, cos_in, sin_in,
    out,
    tok, wq_buf, wo_buf, k_buf, v_buf, acc, qc, k_pick, v_pick, bias, ctx_all, ctx_perm, hop, cos_ref, sin_ref,
    rs_buf, rs_recv,
    tok_sem, own_sem, send_sem, wq_sem, wo_sem, kv_send, kv_sem, ctx_send, ctx_sem,
    move_send, move_sem, keep_sem, hop_send, hop_sem, round_sem, rs_sem, give_send, give_sem,
):
    n_f, n_c, nq, cuts, rs_cols = cfg
    nw = len(cuts)
    chips = n_f // 2
    bits = [1 << i for i in range(chips.bit_length() - 1)]
    levels = len(bits)
    masks = sorted(range(1, chips), key=lambda m: (bin(m).count("1"), m))
    level = {m: bin(m).count("1") for m in masks}
    f = lax.axis_index("fsdp")
    c = lax.axis_index("ctx")
    rows = tok.shape[1]
    depth = tok.shape[2]
    qcols = wq_buf.shape[2]
    qp = qcols // nq
    qh = wq_buf.shape[1] // HALVES
    wo_cols = wo.shape[1]
    t_cols = wo_cols - rs_cols
    rh = wo.shape[0] // HALVES
    wh = wo_buf.shape[1] // HALVES
    part = wo.shape[0] // chips
    ratio = n_f // n_c
    blk_dev = kc.shape[0]
    kv_cols = k_buf.shape[2]
    group = qcols // kv_cols
    n_blocks = k_buf.shape[0]
    q_blocks = rows // BLOCK
    n_list = lists.shape[2]

    def flip(x):
        bit, total = 1, 0
        while bit < n_f:
            total += lax.rem(lax.div(f, bit) + x // bit, 2) * bit
            bit *= 2
        return total

    def peer(x):
        return (flip(x), c)

    sent = []

    def view(kind, ref, s, h):
        if kind == 0:
            return ref.at[pl.ds(h * qh, qh), pl.ds(s * qp, qp)]
        if kind == 2:
            return ref.at[pl.ds(h * rh, rh), pl.ds(0, rs_cols)]
        return ref.at[pl.ds(h * wh, wh), pl.ds(*cuts[s])]

    shard = (wq, wo_buf.at[0], wo)
    bufs = (wq_buf, wo_buf, rs_buf)
    sems = (wq_sem, wo_sem, rs_sem)
    stream = [(0, s) for s in range(nq)] + ([(2, 0)] if rs_cols else []) + [(1, s) for s in range(nw)]
    first_wo = stream.index((1, 0))

    def send(kind, src, slot, s, h, to):
        copy = pltpu.make_async_remote_copy(
            src_ref=src,
            dst_ref=view(kind, bufs[kind].at[slot], s, h),
            send_sem=send_sem.at[len(sent)],
            recv_sem=sems[kind].at[slot, s, h],
            device_id=peer(to),
            device_id_type=MESH,
        )
        copy.start()
        sent.append(copy)

    def arrived(kind, slot, s, h):
        pltpu.make_async_remote_copy(
            src_ref=view(kind, bufs[kind].at[slot], s, h),
            dst_ref=view(kind, bufs[kind].at[slot], s, h),
            send_sem=send_sem.at[0],
            recv_sem=sems[kind].at[slot, s, h],
            device_id=peer(1),
            device_id_type=MESH,
        ).wait_recv()

    def directs(i):
        if i < len(stream):
            kind, s = stream[i]
            for h in range(HALVES):
                for b in bits:
                    send(kind, view(kind, shard[kind], s, h), 2 * b, s, h, 2 * b)

    def to_partner(kind, s):
        for h in range(HALVES):
            send(kind, view(kind, shard[kind], s, h), 1, s, h, 1)

    def pass_level(i, lev):
        if not 0 <= i < len(stream):
            return
        kind, s = stream[i]
        for h in range(HALVES):
            for m in masks:
                if level[m] != lev:
                    continue
                arrived(kind, 2 * m, s, h)
                block = view(kind, bufs[kind].at[2 * m], s, h)
                for b in bits:
                    if not (m & b) and route(m | b, h) == b:
                        send(kind, block, 2 * (m | b), s, h, 2 * b)
                send(kind, block, 2 * m + 1, s, h, 1)

    def kv_copy(which, d):
        other = lax.rem(c + d, n_c)
        src, dst = ((kc, k_buf), (vc, v_buf))[which]
        return pltpu.make_async_remote_copy(
            src_ref=src.at[:, :, pl.ds(pl.multiple_of(other * kv_cols, LANES), kv_cols)],
            dst_ref=dst.at[pl.ds(c * blk_dev, blk_dev)],
            send_sem=kv_send.at[which, d],
            recv_sem=kv_sem.at[which, c],
            device_id=(f, other),
            device_id_type=MESH,
        )

    def kv_wait(which, d):
        plane = lax.rem(c + d, n_c)
        dst = (k_buf, v_buf)[which].at[pl.ds(plane * blk_dev, blk_dev)]
        pltpu.make_async_remote_copy(
            src_ref=dst,
            dst_ref=dst,
            send_sem=kv_send.at[which, d],
            recv_sem=kv_sem.at[which, plane],
            device_id=peer(1),
            device_id_type=MESH,
        ).wait_recv()

    core = lax.rem(f, 2)
    chip = lax.div(f, 2)

    def piece(q):
        return wo.at[pl.ds(pl.multiple_of(q * part, part), part), pl.ds(rs_cols, t_cols)]

    def hop_copy(q, source):
        return pltpu.make_async_remote_copy(
            src_ref=piece(q),
            dst_ref=hop.at[source],
            send_sem=hop_send.at[q],
            recv_sem=hop_sem.at[source],
            device_id=(q * 2 + core, c),
            device_id_type=MESH,
        )

    def move_dst(i, plane):
        return wo_buf.at[
            0,
            pl.ds(pl.multiple_of(plane * part, part), part),
            pl.ds(pl.multiple_of(i * t_cols, t_cols), t_cols),
        ]

    def owner(p):
        source = p * 2 + core
        return lax.div(source, ratio), lax.div(lax.rem(source, ratio), 2)

    def move(src, p):
        home, i = owner(p)
        return pltpu.make_async_remote_copy(
            src_ref=src,
            dst_ref=move_dst(i, c),
            send_sem=move_send.at[p],
            recv_sem=move_sem.at[i, c],
            device_id=(f, home),
            device_id_type=MESH,
        )

    def keep(src, p):
        _, i = owner(p)
        return pltpu.make_async_copy(src, move_dst(i, c), keep_sem.at[i])

    def forward(src, p):
        home, _ = owner(p)

        @pl.when(home == c)
        def _():
            keep(src, p).start()

        @pl.when(home != c)
        def _():
            move(src, p).start()

    def start_moves():
        forward(piece(chip), chip)

        @pl.loop(1, chips)
        def _(d):
            p = lax.rem(chip + d, chips)
            hop_copy(p, p).wait_recv()
            forward(hop.at[p], p)

    def wait_moves():
        for i in range(ratio // 2):
            keep(piece(chip), lax.div(c * ratio + 2 * i, 2)).wait()

            @pl.loop(1, n_c)
            def _(d):
                plane = lax.rem(c + d, n_c)
                pltpu.make_async_remote_copy(
                    src_ref=move_dst(i, plane),
                    dst_ref=move_dst(i, plane),
                    send_sem=move_send.at[0],
                    recv_sem=move_sem.at[i, plane],
                    device_id=peer(1),
                    device_id_type=MESH,
                ).wait_recv()

    def ctx_view(s, origin):
        return ctx_all.at[origin, :, pl.ds(s * qp, qp)]

    def ctx_copy(s, origin, side, src):
        return pltpu.make_async_remote_copy(
            src_ref=src,
            dst_ref=ctx_view(s, origin),
            send_sem=ctx_send.at[s, origin, side],
            recv_sem=ctx_sem.at[s, origin],
            device_id=(f, c + 1 if side else c - 1),
            device_id_type=MESH,
        )

    def ctx_start(s):
        own = qc.at[:, pl.ds(s * qp, qp)]

        @pl.when(c + 1 < n_c)
        def _():
            ctx_copy(s, c, 1, own).start()

        @pl.when(c > 0)
        def _():
            ctx_copy(s, c, 0, own).start()

        ctx_all[c, :, s * qp:(s + 1) * qp] = qc[:, s * qp:(s + 1) * qp]

    def ctx_pass(s, d):
        below = c - d
        above = c + d

        @pl.when(below >= 0)
        def _():
            ctx_copy(s, below, 0, ctx_view(s, below)).wait_recv()

            @pl.when(c + 1 < n_c)
            def _():
                ctx_copy(s, below, 1, ctx_view(s, below)).start()

        @pl.when(above < n_c)
        def _():
            ctx_copy(s, above, 1, ctx_view(s, above)).wait_recv()

            @pl.when(c > 0)
            def _():
                ctx_copy(s, above, 0, ctx_view(s, above)).start()

    def ctx_drain(s):
        @pl.loop(0, n_c)
        def _(origin):
            @pl.when(jnp.logical_and(origin <= c, c + 1 < n_c))
            def _():
                ctx_copy(s, origin, 1, ctx_view(s, origin)).wait_send()

            @pl.when(jnp.logical_and(origin >= c, c > 0))
            def _():
                ctx_copy(s, origin, 0, ctx_view(s, origin)).wait_send()

    tile = min(256, qp)

    def q_part(j, s):
        for t in range(qp // tile):
            cols = slice(s * qp + t * tile, s * qp + (t + 1) * tile)
            acc[:, cols] += jnp.dot(tok[j], wq_buf[j, :, cols], preferred_element_type=jnp.float32)

    def attend(s):
        first = s * qp // HEAD
        heads = range(first, first + qp // HEAD)
        for h in heads:
            cols = slice(h * HEAD, (h + 1) * HEAD)
            x = acc[:, cols]
            turned = x * cos_ref[...] + pltpu.roll(x, HEAD // 2, 1) * sin_ref[...]
            qc[:, cols] = turned.astype(jnp.bfloat16)

        @pl.loop(0, q_blocks)
        def _(b):
            q_rows = pl.ds(pl.multiple_of(b * BLOCK, BLOCK), BLOCK)
            own_block = n_blocks - q_blocks + b
            later = lax.broadcasted_iota(jnp.int32, (BLOCK, BLOCK), 1) > lax.broadcasted_iota(
                jnp.int32, (BLOCK, BLOCK), 0
            )
            for n in range(n_list):
                entry = lists[0, b, n]
                hide = jnp.where(entry == own_block, -jnp.inf, 0.0)
                bias[:, n * BLOCK:(n + 1) * BLOCK] = jnp.where(later, hide, 0.0)
            for g in sorted({h // group for h in heads}):
                head_cols = slice(g * HEAD, (g + 1) * HEAD)
                for n in range(n_list):
                    entry = lists[0, b, n]
                    k_pick[n * BLOCK:(n + 1) * BLOCK, :] = k_buf[entry, :, head_cols]
                    v_pick[n * BLOCK:(n + 1) * BLOCK, :] = v_buf[entry, :, head_cols]
                for h in heads:
                    if h // group != g:
                        continue
                    cols = slice(h * HEAD, (h + 1) * HEAD)
                    scores = lax.dot_general(
                        qc[q_rows, cols], k_pick[...], (((1,), (1,)), ((), ())),
                        preferred_element_type=jnp.float32,
                    ) + bias[...]
                    top = jnp.max(scores, axis=1, keepdims=True)
                    raised = jnp.exp(scores - top)
                    total = jnp.sum(raised, axis=1, keepdims=True)
                    mixed = jnp.dot(
                        raised.astype(jnp.bfloat16), v_pick[...], preferred_element_type=jnp.float32
                    )
                    qc[q_rows, cols] = (mixed / total).astype(jnp.bfloat16)

    def share(j, s):
        target = flip(j)
        first, width = cuts[s]
        i, offset = divmod(first, t_cols)
        start = pl.multiple_of((2 * i + lax.rem(target, 2)) * wo_cols + rs_cols + offset, LANES)
        acc[:, pl.ds(start, width)] += jnp.dot(
            ctx_perm[lax.div(target, 2)], wo_buf[j, :, first:first + width],
            preferred_element_type=jnp.float32,
        )

    def out_cols(s, k):
        if s == nw:
            return pl.ds(k * wo_cols, rs_cols)
        first, width = cuts[s]
        i, offset = divmod(first, t_cols)
        return pl.ds((2 * i + k) * wo_cols + rs_cols + offset, width)

    def gift(home, k):
        return tok.at[home, :, pl.ds(k * rs_cols, rs_cols)]

    def give(home, k, side):
        slot = jnp.where(home == c + 2 * side - 1, n_c * (1 - side) + home * side, home)
        return pltpu.make_async_remote_copy(
            src_ref=gift(home, k),
            dst_ref=rs_recv.at[slot, k],
            send_sem=give_send.at[home, k],
            recv_sem=give_sem.at[slot, k],
            device_id=(f, c + 2 * side - 1),
            device_id_type=MESH,
        )

    def got(slot, k):
        pltpu.make_async_remote_copy(
            src_ref=rs_recv.at[slot, k],
            dst_ref=rs_recv.at[slot, k],
            send_sem=give_send.at[0, k],
            recv_sem=give_sem.at[slot, k],
            device_id=peer(1),
            device_id_type=MESH,
        ).wait_recv()

    def rs_start():
        locals_in[5].wait()

        @pl.loop(0, n_f)
        def _(j):
            @pl.when(lax.rem(j, 2) == 1)
            def _():
                for h in range(HALVES):
                    arrived(2, j, 0, h)

            target = flip(j)
            cols = pl.ds(pl.multiple_of(lax.rem(target, 2) * rs_cols, LANES), rs_cols)
            tok[lax.div(target, 2), :, cols] = jnp.dot(
                qc[...], rs_buf[j], preferred_element_type=jnp.float32
            ).astype(jnp.bfloat16)

        @pl.when(c == 0)
        def _():
            for home in range(n_c - 1, 0, -1):
                for k in range(2):
                    give(home, k, 1).start()

        @pl.when(c == n_c - 1)
        def _():
            for home in range(n_c - 1):
                for k in range(2):
                    give(home, k, 0).start()

    def rs_pass(e, k):
        def add(home, side):
            got(home, k)
            cols = slice(k * rs_cols, (k + 1) * rs_cols)
            tok[home, :, cols] = (
                tok[home, :, cols].astype(jnp.float32) + rs_recv[home, k].astype(jnp.float32)
            ).astype(jnp.bfloat16)
            give(home, k, side).start()

        @pl.when(jnp.logical_and(c > 0, c + e < n_c))
        def _():
            add(c + e, 1)

        @pl.when(jnp.logical_and(c < n_c - 1, c - e >= 0))
        def _():
            add(c - e, 0)

    def take():
        for k in range(2):
            cols = slice(k * rs_cols, (k + 1) * rs_cols)
            place = out_cols(nw, k)
            acc[:, place] = tok[c, :, cols].astype(jnp.float32)

            @pl.when(c > 0)
            def _():
                got(c, k)
                acc[:, place] += rs_recv[c, k].astype(jnp.float32)

            @pl.when(c < n_c - 1)
            def _():
                got(n_c, k)
                acc[:, place] += rs_recv[n_c, k].astype(jnp.float32)

            out[:, place] = acc[:, place].astype(jnp.bfloat16)

    last_slot = 2 * min(m for m in masks if level[m] == levels)

    def shares(s, start, stop):
        @pl.loop(start, stop)
        def _(j):
            @pl.when(lax.rem(j, 2) == 1)
            def _():
                for h in range(HALVES):
                    arrived(1, j, s, h)

            share(j, s)

    def compute_early(i):
        kind, s = stream[i]
        if kind == 1 and levels > 1:
            shares(s, 0, 4)
            if levels == 2:
                shares(s, 4, last_slot)

    def compute(i):
        kind, s = stream[i]
        if kind == 0:
            @pl.loop(2, n_f)
            def _(j):
                @pl.when(lax.rem(j, 2) == 1)
                def _():
                    for h in range(HALVES):
                        arrived(0, j, s, h)

                q_part(j, s)

            attend(s)
            ctx_start(s)
            return
        shares(s, (last_slot if levels == 2 else 4) if levels > 1 else 0, n_f)
        for k in range(2):
            cols = out_cols(s, k)
            out[:, cols] = acc[:, cols].astype(jnp.bfloat16)

    def tok_copy(j):
        start = pl.multiple_of(flip(j) * depth, LANES)
        return pltpu.make_async_copy(tokens.at[:, pl.ds(start, depth)], tok.at[j], tok_sem.at[j])

    mine = pl.ds(pl.multiple_of(c * kv_cols, LANES), kv_cols)
    locals_in = [
        pltpu.make_async_copy(wq, wq_buf.at[0], own_sem.at[0]),
        pltpu.make_async_copy(kc.at[:, :, mine], k_buf.at[pl.ds(c * blk_dev, blk_dev)], own_sem.at[1]),
        pltpu.make_async_copy(vc.at[:, :, mine], v_buf.at[pl.ds(c * blk_dev, blk_dev)], own_sem.at[2]),
        pltpu.make_async_copy(cos_in, cos_ref, own_sem.at[3]),
        pltpu.make_async_copy(sin_in, sin_ref, own_sem.at[4]),
    ]
    if rs_cols:
        locals_in.append(pltpu.make_async_copy(wo.at[:, pl.ds(0, rs_cols)], rs_buf.at[0], own_sem.at[5]))

    barrier = pltpu.get_barrier_semaphore()

    def beside(sem, extra):
        for b in extra + [2 * b for b in bits]:
            pl.semaphore_signal(sem, inc=1, device_id=peer(b), device_id_type=MESH)

        @pl.when(c > 0)
        def _():
            pl.semaphore_signal(sem, inc=1, device_id=(f, c - 1), device_id_type=MESH)

        @pl.when(c < n_c - 1)
        def _():
            pl.semaphore_signal(sem, inc=1, device_id=(f, c + 1), device_id_type=MESH)

    near = len(bits) + jnp.where(c > 0, 1, 0) + jnp.where(c < n_c - 1, 1, 0)
    beside(barrier, [1])
    for copy in locals_in:
        copy.start()
    for j in range(n_f):
        tok_copy(j).start()
    acc[...] = jnp.zeros_like(acc)
    pl.semaphore_wait(barrier, near + 1)
    rounds = max(levels, n_c - 1) - 1

    def kv_start(d):
        @pl.when(c + d < n_c)
        def _():
            for which in range(2):
                kv_copy(which, d).start()

        @pl.when(c - d >= 0)
        def _():
            for which in range(2):
                kv_copy(which, n_c - d).start()

    def hops(lev):
        for m in masks:
            if level[m] == lev:
                hop_copy(lax.div(flip(2 * m), 2), chip).start()

    beside(round_sem.at[0], [])
    hops(1)
    kv_start(1)
    for r in range(rounds):
        pl.semaphore_wait(round_sem.at[r], near)
        if r + 1 < rounds:
            beside(round_sem.at[r + 1], [])
        hops(r + 2)
        if r + 2 < n_c:
            kv_start(r + 2)
        if r == 0:
            for i in range(AHEAD):
                directs(i)
    for s in range(nq):
        to_partner(0, s)
    if rs_cols:
        to_partner(2, 0)

    locals_in[0].wait()
    for j in range(n_f):
        tok_copy(j).wait()
    start_moves()
    for s in range(nq):
        for h in range(HALVES):
            arrived(0, 1, s, h)

        @pl.loop(0, 2)
        def _(j):
            q_part(j, s)

    for copy in locals_in[1:5]:
        copy.wait()

    lag = levels - 1
    total = len(stream)
    done = {}
    queued = AHEAD

    def ctx_next(s):
        if done[s] < n_c:
            ctx_pass(s, done[s])
            done[s] += 1

    for step in range(total + lag):
        pass_level(step, 1)
        i = step - lag
        while queued < total and queued <= step + AHEAD and not (rs_cols and step == nq - 1 and queued > nq):
            directs(queued)
            queued += 1
        for lev in range(2, levels):
            pass_level(step - lev + 1, lev)
        for s in range(nq):
            if s in done and not (rs_cols and s == nq - 1):
                ctx_next(s)
        if rs_cols and step == nq + 1:
            for k in range(2):
                for e in range(n_c - 2, 1, -1):
                    rs_pass(e, k)
                ctx_next(nq - 1)
        if i == first_wo:
            for s in range(nq):
                while done[s] < n_c:
                    ctx_next(s)
            for q in range(chips):
                for plane in range(n_c):
                    ctx_perm[q, :, plane * part:(plane + 1) * part] = ctx_all[
                        plane, :, q * part:(q + 1) * part
                    ]
        if i >= 0 and stream[i][0] != 2:
            if levels > 1:
                compute_early(i)
                if rs_cols and step == total + lag - 1:
                    take()
                pass_level(i, levels)
            if i == 0:
                @pl.loop(1, n_c)
                def _(d):
                    for which in range(2):
                        kv_wait(which, d)
            compute(i)
            if stream[i][0] == 0:
                done[stream[i][1]] = 1
            if i == nq - 1:
                if rs_cols:
                    pass_level(nq, 2)
                    rs_start()
                acc[...] = jnp.zeros_like(acc)
                ctx_next(nq - 1)
            if rs_cols and i == first_wo:
                for k in range(2):
                    rs_pass(1, k)
        if step + 1 + AHEAD == max(first_wo, AHEAD + 1):
            wait_moves()
            for s in range(nw):
                to_partner(1, s)

    assert len(sent) == send_sem.shape[0]
    for copy in sent:
        copy.wait_send()

    @pl.loop(1, n_c)
    def _(d):
        for which in range(2):
            kv_copy(which, d).wait_send()

    for s in range(nq):
        ctx_drain(s)

    @pl.loop(0, chips)
    def _(q):
        @pl.when(q != chip)
        def _():
            hop_copy(q, chip).wait_send()

        home, _ = owner(q)

        @pl.when(home != c)
        def _():
            move(piece(chip), q).wait_send()

    if rs_cols:
        for k in range(2):
            @pl.loop(0, n_c)
            def _(home):
                @pl.when(home != c)
                def _():
                    give(home, k, jnp.where(home > c, 1, 0)).wait_send()


def body(n_f, n_c, tokens, wq, wo, key_cache, value_cache, key_blocks):
    rows, width = tokens.shape
    depth = width // n_f
    qcols = wq.shape[1]
    cache = key_cache.shape[0]
    blk_dev = cache // BLOCK
    kv_cols = key_cache.shape[1] // n_c
    n_list = key_blocks.shape[2]
    cosine, sine = tables(rows, cache * n_c)
    nq = max(1, min(4, qcols // HEAD))
    ratio = n_f // n_c
    chips = n_f // 2
    part = wo.shape[0] // chips
    rs_cols = wo.shape[1] // 4 if ratio == 2 and n_f == chips * 2 == n_c * 2 and chips.bit_length() == 3 and wo.shape[1] % (4 * LANES) == 0 else 0
    t_cols = wo.shape[1] - rs_cols
    moved = (part * n_c, t_cols * ratio // 2)
    if rs_cols:
        widths = [rs_cols] * (moved[1] // rs_cols)
    else:
        parts = max(1, min(4, moved[1] // LANES))
        widths = [moved[1] // parts] * parts
    cuts = tuple((sum(widths[:s]), w) for s, w in enumerate(widths))
    nw = len(cuts)
    rs_shape = (wo.shape[0], rs_cols) if rs_cols else (16, LANES)
    share_shape = (n_c + 1, 2, rows, rs_cols) if rs_cols else (1, 1, 16, LANES)
    any_spec = pl.BlockSpec(memory_space=pl.ANY)
    bf16 = jnp.bfloat16
    f32 = jnp.float32
    dma = pltpu.SemaphoreType.DMA
    return pl.pallas_call(
        functools.partial(kernel, (n_f, n_c, nq, cuts, rs_cols)),
        out_shape=pltpu.VMEM((rows, width // n_c), bf16),
        in_specs=[pl.BlockSpec(memory_space=pltpu.SMEM)] + [any_spec] * 7,
        out_specs=pl.BlockSpec(memory_space=pltpu.VMEM),
        scratch_shapes=[
            pltpu.VMEM((n_f, rows, depth), bf16),
            pltpu.VMEM((n_f,) + wq.shape, bf16),
            pltpu.VMEM((n_f,) + moved, bf16),
            pltpu.VMEM((blk_dev * n_c, BLOCK, kv_cols), bf16),
            pltpu.VMEM((blk_dev * n_c, BLOCK, kv_cols), bf16),
            pltpu.VMEM((rows, max(qcols, width // n_c)), f32),
            pltpu.VMEM((rows, qcols), bf16),
            pltpu.VMEM((n_list * BLOCK, HEAD), bf16),
            pltpu.VMEM((n_list * BLOCK, HEAD), bf16),
            pltpu.VMEM((BLOCK, n_list * BLOCK), f32),
            pltpu.VMEM((n_c, rows, qcols), bf16),
            pltpu.VMEM((chips, rows, n_c * part), bf16),
            pltpu.VMEM((chips, part, t_cols), bf16),
            pltpu.VMEM((rows, HEAD), f32),
            pltpu.VMEM((rows, HEAD), f32),
            pltpu.VMEM((n_f if rs_cols else 1,) + rs_shape, bf16),
            pltpu.VMEM(share_shape, bf16),
            dma((n_f,)),
            dma((6,)),
            dma(((nq + nw + (1 if rs_cols else 0)) * HALVES * (n_f - 1),)),
            dma((n_f, nq, HALVES)),
            dma((n_f, nw, HALVES)),
            dma((2, n_c)),
            dma((2, n_c)),
            dma((nq, n_c, 2)),
            dma((nq, n_c)),
            dma((chips,)),
            dma((ratio // 2, n_c)),
            dma((ratio // 2,)),
            dma((chips,)),
            dma((chips,)),
            pltpu.SemaphoreType.REGULAR((max(chips.bit_length() - 1, n_c - 1),)),
            dma((n_f, 1, HALVES)),
            dma((n_c, 2)),
            dma((n_c + 1, 2)),
        ],
        compiler_params=pltpu.CompilerParams(
            collective_id=0, has_side_effects=True, vmem_limit_bytes=67043328 - 2 * rows * width // n_c - 65536
        ),
    )(
        key_blocks,
        tokens,
        wq,
        wo,
        key_cache.reshape(blk_dev, BLOCK, key_cache.shape[1]),
        value_cache.reshape(blk_dev, BLOCK, value_cache.shape[1]),
        jnp.asarray(cosine, jnp.float32),
        jnp.asarray(sine, jnp.float32),
    )


def solution(mesh):
    in_specs = (
        P("fsdp", None),
        P("fsdp", "ctx"),
        P("ctx", "fsdp"),
        P(("fsdp", "ctx"), None),
        P(("fsdp", "ctx"), None),
        P("fsdp", None, None),
    )
    step = functools.partial(body, mesh.shape["fsdp"], mesh.shape["ctx"])
    return jax.shard_map(
        step, mesh=mesh, in_specs=in_specs, out_specs=P("fsdp", "ctx"), check_vma=False
    )
```

```python
import functools

import jax
import jax.numpy as jnp
import numpy as np
from jax import lax
from jax.experimental import pallas as pl
from jax.experimental.pallas import tpu as pltpu
from jax.sharding import PartitionSpec as P

HEAD = 128
BLOCK = 128
LANES = 128
AHEAD = 2
HALVES = 2
MESH = pl.DeviceIdType.MESH

rope_base = 1000000.0


def tables(row_count, key_total):
    half_width = HEAD // 2
    exponent = -(np.arange(half_width, dtype=np.float32) * np.float32(2.0)) / np.float32(HEAD)
    frequency = np.power(np.float32(rope_base), exponent, dtype=np.float32)
    positions = (key_total - row_count + np.arange(row_count)).astype(np.float32)
    angles = positions[:, None] * frequency[None, :]
    scale = np.float32(HEAD ** (-0.5))
    cosine = np.cos(angles) * scale
    sine = np.sin(angles) * scale
    return np.concatenate([cosine, cosine], axis=1), np.concatenate([-sine, sine], axis=1)


def low_bit(m):
    return m & -m


def high_bit(m):
    return 1 << (m.bit_length() - 1)


def route(mask, half):
    return low_bit(mask) if half % 2 == 0 else high_bit(mask)


def kernel(
    cfg,
    lists, tokens, wq, wo, kc, vc, cos_in, sin_in,
    out,
    tok, wq_buf, wo_buf, k_buf, v_buf, acc, qc, k_pick, v_pick, bias, ctx_all, ctx_perm, hop, cos_ref, sin_ref,
    rs_buf, rs_recv, pair_buf, pair_hop,
    tok_sem, own_sem, send_sem, wq_sem, wo_sem, kv_send, kv_sem, ctx_send, ctx_sem,
    move_send, move_sem, keep_sem, hop_send, hop_sem, round_sem, rs_sem, give_send, give_sem,
    pair_src_send, pair_src_sem, pair_move_send, pair_move_sem, pair_keep, pair_send, pair_sem, pair_own_send, pair_own_sem,
):
    n_f, n_c, nq, cuts, rs_cols, pair_cols = cfg
    nw = len(cuts)
    chips = n_f // 2
    bits = [1 << i for i in range(chips.bit_length() - 1)]
    levels = len(bits)
    masks = sorted(range(1, chips), key=lambda m: (bin(m).count("1"), m))
    level = {m: bin(m).count("1") for m in masks}
    f = lax.axis_index("fsdp")
    c = lax.axis_index("ctx")
    rows = tok.shape[1]
    depth = tok.shape[2]
    qcols = wq_buf.shape[2]
    qp = qcols // nq
    qh = wq_buf.shape[1] // HALVES
    wo_cols = wo.shape[1]
    t_cols = wo_cols - rs_cols - pair_cols
    rh = wo.shape[0] // HALVES
    wh = wo_buf.shape[1] // HALVES
    part = wo.shape[0] // chips
    ratio = n_f // n_c
    blk_dev = kc.shape[0]
    kv_cols = k_buf.shape[2]
    group = qcols // kv_cols
    n_blocks = k_buf.shape[0]
    q_blocks = rows // BLOCK
    n_list = lists.shape[2]

    def flip(x):
        bit, total = 1, 0
        while bit < n_f:
            total += lax.rem(lax.div(f, bit) + x // bit, 2) * bit
            bit *= 2
        return total

    def peer(x):
        return (flip(x), c)

    sent = []

    def view(kind, ref, s, h):
        if kind == 0:
            return ref.at[pl.ds(h * qh, qh), pl.ds(s * qp, qp)]
        if kind == 2:
            return ref.at[pl.ds(h * rh, rh), pl.ds(0, rs_cols)]
        return ref.at[pl.ds(h * wh, wh), pl.ds(*cuts[s])]

    shard = (wq, wo_buf.at[0], wo)
    bufs = (wq_buf, wo_buf, rs_buf)
    sems = (wq_sem, wo_sem, rs_sem)
    stream = [(0, s) for s in range(nq)] + ([(2, 0)] if rs_cols else []) + [(1, s) for s in range(nw)]
    stream += [(3, 0)] if pair_cols else []
    first_wo = stream.index((1, 0))

    def send(kind, src, slot, s, h, to):
        copy = pltpu.make_async_remote_copy(
            src_ref=src,
            dst_ref=view(kind, bufs[kind].at[slot], s, h),
            send_sem=send_sem.at[len(sent)],
            recv_sem=sems[kind].at[slot, s, h],
            device_id=peer(to),
            device_id_type=MESH,
        )
        copy.start()
        sent.append(copy)

    def arrived(kind, slot, s, h):
        pltpu.make_async_remote_copy(
            src_ref=view(kind, bufs[kind].at[slot], s, h),
            dst_ref=view(kind, bufs[kind].at[slot], s, h),
            send_sem=send_sem.at[0],
            recv_sem=sems[kind].at[slot, s, h],
            device_id=peer(1),
            device_id_type=MESH,
        ).wait_recv()

    def directs(i):
        if i < len(stream):
            kind, s = stream[i]
            if kind == 3:
                pair_exchange()
                return
            for h in range(HALVES):
                for b in bits:
                    send(kind, view(kind, shard[kind], s, h), 2 * b, s, h, 2 * b)

    def to_partner(kind, s):
        for h in range(HALVES):
            send(kind, view(kind, shard[kind], s, h), 1, s, h, 1)

    def pass_level(i, lev):
        if not 0 <= i < len(stream):
            return
        kind, s = stream[i]
        if kind == 3:
            if lev == 1:
                pair_arrive()
            return
        for h in range(HALVES):
            for m in masks:
                if level[m] != lev:
                    continue
                arrived(kind, 2 * m, s, h)
                block = view(kind, bufs[kind].at[2 * m], s, h)
                for b in bits:
                    if not (m & b) and route(m | b, h) == b:
                        send(kind, block, 2 * (m | b), s, h, 2 * b)
                send(kind, block, 2 * m + 1, s, h, 1)

    def kv_copy(which, d):
        other = lax.rem(c + d, n_c)
        src, dst = ((kc, k_buf), (vc, v_buf))[which]
        return pltpu.make_async_remote_copy(
            src_ref=src.at[:, :, pl.ds(pl.multiple_of(other * kv_cols, LANES), kv_cols)],
            dst_ref=dst.at[pl.ds(c * blk_dev, blk_dev)],
            send_sem=kv_send.at[which, d],
            recv_sem=kv_sem.at[which, c],
            device_id=(f, other),
            device_id_type=MESH,
        )

    def kv_wait(which, d):
        plane = lax.rem(c + d, n_c)
        dst = (k_buf, v_buf)[which].at[pl.ds(plane * blk_dev, blk_dev)]
        pltpu.make_async_remote_copy(
            src_ref=dst,
            dst_ref=dst,
            send_sem=kv_send.at[which, d],
            recv_sem=kv_sem.at[which, plane],
            device_id=peer(1),
            device_id_type=MESH,
        ).wait_recv()

    core = lax.rem(f, 2)
    chip = lax.div(f, 2)

    def piece(q):
        return wo.at[pl.ds(pl.multiple_of(q * part, part), part), pl.ds(rs_cols, t_cols)]

    def hop_copy(q, source):
        return pltpu.make_async_remote_copy(
            src_ref=piece(q),
            dst_ref=hop.at[source],
            send_sem=hop_send.at[q],
            recv_sem=hop_sem.at[source],
            device_id=(q * 2 + core, c),
            device_id_type=MESH,
        )

    def move_dst(i, plane):
        return wo_buf.at[
            0,
            pl.ds(pl.multiple_of(plane * part, part), part),
            pl.ds(pl.multiple_of(i * t_cols, t_cols), t_cols),
        ]

    def owner(p):
        source = p * 2 + core
        return lax.div(source, ratio), lax.div(lax.rem(source, ratio), 2)

    def move(src, p):
        home, i = owner(p)
        return pltpu.make_async_remote_copy(
            src_ref=src,
            dst_ref=move_dst(i, c),
            send_sem=move_send.at[p],
            recv_sem=move_sem.at[i, c],
            device_id=(f, home),
            device_id_type=MESH,
        )

    def keep(src, p):
        _, i = owner(p)
        return pltpu.make_async_copy(src, move_dst(i, c), keep_sem.at[i])

    def forward(src, p):
        home, _ = owner(p)

        @pl.when(home == c)
        def _():
            keep(src, p).start()

        @pl.when(home != c)
        def _():
            move(src, p).start()

    def start_moves():
        forward(piece(chip), chip)

        @pl.loop(1, chips)
        def _(d):
            p = lax.rem(chip + d, chips)
            hop_copy(p, p).wait_recv()
            forward(hop.at[p], p)

    def wait_moves():
        for i in range(ratio // 2):
            keep(piece(chip), lax.div(c * ratio + 2 * i, 2)).wait()

            @pl.loop(1, n_c)
            def _(d):
                plane = lax.rem(c + d, n_c)
                pltpu.make_async_remote_copy(
                    src_ref=move_dst(i, plane),
                    dst_ref=move_dst(i, plane),
                    send_sem=move_send.at[0],
                    recv_sem=move_sem.at[i, plane],
                    device_id=peer(1),
                    device_id_type=MESH,
                ).wait_recv()

    def ctx_view(s, origin):
        return ctx_all.at[origin, :, pl.ds(s * qp, qp)]

    def ctx_copy(s, origin, side, src):
        return pltpu.make_async_remote_copy(
            src_ref=src,
            dst_ref=ctx_view(s, origin),
            send_sem=ctx_send.at[s, origin, side],
            recv_sem=ctx_sem.at[s, origin],
            device_id=(f, c + 1 if side else c - 1),
            device_id_type=MESH,
        )

    def ctx_start(s):
        own = qc.at[:, pl.ds(s * qp, qp)]

        @pl.when(c + 1 < n_c)
        def _():
            ctx_copy(s, c, 1, own).start()

        @pl.when(c > 0)
        def _():
            ctx_copy(s, c, 0, own).start()

        ctx_all[c, :, s * qp:(s + 1) * qp] = qc[:, s * qp:(s + 1) * qp]

    def ctx_pass(s, d):
        below = c - d
        above = c + d

        @pl.when(below >= 0)
        def _():
            ctx_copy(s, below, 0, ctx_view(s, below)).wait_recv()

            @pl.when(c + 1 < n_c)
            def _():
                ctx_copy(s, below, 1, ctx_view(s, below)).start()

        @pl.when(above < n_c)
        def _():
            ctx_copy(s, above, 1, ctx_view(s, above)).wait_recv()

            @pl.when(c > 0)
            def _():
                ctx_copy(s, above, 0, ctx_view(s, above)).start()

    def ctx_drain(s):
        @pl.loop(0, n_c)
        def _(origin):
            @pl.when(jnp.logical_and(origin <= c, c + 1 < n_c))
            def _():
                ctx_copy(s, origin, 1, ctx_view(s, origin)).wait_send()

            @pl.when(jnp.logical_and(origin >= c, c > 0))
            def _():
                ctx_copy(s, origin, 0, ctx_view(s, origin)).wait_send()

    tile = min(256, qp)

    def q_part(j, s):
        for t in range(qp // tile):
            cols = slice(s * qp + t * tile, s * qp + (t + 1) * tile)
            acc[:, cols] += jnp.dot(tok[j], wq_buf[j, :, cols], preferred_element_type=jnp.float32)

    def attend(s):
        first = s * qp // HEAD
        heads = range(first, first + qp // HEAD)
        for h in heads:
            cols = slice(h * HEAD, (h + 1) * HEAD)
            x = acc[:, cols]
            turned = x * cos_ref[...] + pltpu.roll(x, HEAD // 2, 1) * sin_ref[...]
            qc[:, cols] = turned.astype(jnp.bfloat16)

        @pl.loop(0, q_blocks)
        def _(b):
            q_rows = pl.ds(pl.multiple_of(b * BLOCK, BLOCK), BLOCK)
            own_block = n_blocks - q_blocks + b
            later = lax.broadcasted_iota(jnp.int32, (BLOCK, BLOCK), 1) > lax.broadcasted_iota(
                jnp.int32, (BLOCK, BLOCK), 0
            )
            for n in range(n_list):
                entry = lists[0, b, n]
                hide = jnp.where(entry == own_block, -jnp.inf, 0.0)
                bias[:, n * BLOCK:(n + 1) * BLOCK] = jnp.where(later, hide, 0.0)
            for g in sorted({h // group for h in heads}):
                head_cols = slice(g * HEAD, (g + 1) * HEAD)
                for n in range(n_list):
                    entry = lists[0, b, n]
                    k_pick[n * BLOCK:(n + 1) * BLOCK, :] = k_buf[entry, :, head_cols]
                    v_pick[n * BLOCK:(n + 1) * BLOCK, :] = v_buf[entry, :, head_cols]
                for h in heads:
                    if h // group != g:
                        continue
                    cols = slice(h * HEAD, (h + 1) * HEAD)
                    scores = lax.dot_general(
                        qc[q_rows, cols], k_pick[...], (((1,), (1,)), ((), ())),
                        preferred_element_type=jnp.float32,
                    ) + bias[...]
                    top = jnp.max(scores, axis=1, keepdims=True)
                    raised = jnp.exp(scores - top)
                    total = jnp.sum(raised, axis=1, keepdims=True)
                    mixed = jnp.dot(
                        raised.astype(jnp.bfloat16), v_pick[...], preferred_element_type=jnp.float32
                    )
                    qc[q_rows, cols] = (mixed / total).astype(jnp.bfloat16)

    def share(j, s):
        target = flip(j)
        first, width = cuts[s]
        i, offset = divmod(first, t_cols)
        start = pl.multiple_of((2 * i + lax.rem(target, 2)) * wo_cols + rs_cols + offset, LANES)
        acc[:, pl.ds(start, width)] += jnp.dot(
            ctx_perm[lax.div(target, 2)], wo_buf[j, :, first:first + width],
            preferred_element_type=jnp.float32,
        )

    def out_cols(s, k):
        if s > nw:
            return pl.ds(k * wo_cols + rs_cols + t_cols, pair_cols)
        if s == nw:
            return pl.ds(k * wo_cols, rs_cols)
        first, width = cuts[s]
        i, offset = divmod(first, t_cols)
        return pl.ds((2 * i + k) * wo_cols + rs_cols + offset, width)

    strip = wo.shape[0] // 4
    y_of = (0, 0, 3, 3)
    x_of = (1, 2, 1, 2)

    def quarter(q):
        return wo.at[pl.ds(q * strip, strip), pl.ds(rs_cols + t_cols, pair_cols)]

    def pair_source(index, src, m, which, to):
        return pltpu.make_async_remote_copy(
            src_ref=src,
            dst_ref=pair_hop.at[m - 1, which],
            send_sem=pair_src_send.at[index],
            recv_sem=pair_src_sem.at[m - 1, which],
            device_id=peer(to),
            device_id_type=MESH,
        )

    def pair_sources():
        return [
            pair_source(0, quarter(2), 1, 1, 2),
            pair_source(1, quarter(3), 2, 0, 4),
            pair_source(2, quarter(0), 1, 0, 2),
            pair_source(3, quarter(1), 2, 1, 4),
            pair_source(4, pair_hop.at[0, 1], 3, 1, 4),
            pair_source(5, pair_hop.at[1, 0], 3, 0, 2),
        ]

    def pair_move(m, which):
        home = lax.div(flip(2 * m), 2)
        q = (y_of, x_of)[which][m]
        src = quarter(q) if m == 0 else pair_hop.at[m - 1, which]
        dst = pair_buf.at[0, q, pl.ds(pl.multiple_of(c * strip, strip), strip), :]
        stay = pltpu.make_async_copy(src, dst, pair_keep.at[which])
        go = pltpu.make_async_remote_copy(
            src_ref=src,
            dst_ref=dst,
            send_sem=pair_move_send.at[m, which],
            recv_sem=pair_move_sem.at[which, c],
            device_id=(f, home),
            device_id_type=MESH,
        )
        return home, stay, go

    def pair_moves(m):
        for which in range(2):
            home, stay, go = pair_move(m, which)

            @pl.when(home == c)
            def _():
                stay.start()

            @pl.when(home != c)
            def _():
                go.start()

    def pair_forward():
        sources = pair_sources()
        sources[0].wait_recv()
        sources[4].start()
        sources[1].wait_recv()
        sources[5].start()

    def pair_rest():
        sources = pair_sources()
        pair_moves(0)
        sources[2].wait_recv()
        pair_moves(1)
        sources[3].wait_recv()
        pair_moves(2)

    def pair_far():
        sources = pair_sources()
        sources[4].wait_recv()
        sources[5].wait_recv()
        pair_moves(3)

    def held(which):
        side = lax.rem(lax.rem(chip, 2) + lax.rem(c, 2), 2)
        if which == 1:
            return side + 1
        return lax.rem(lax.div(chip, 2) + lax.div(c, 2), 2) * 3

    def pair_swap(which):
        q = held(which)
        return pltpu.make_async_remote_copy(
            src_ref=pair_buf.at[0, q],
            dst_ref=pair_buf.at[0, q],
            send_sem=pair_send.at[which],
            recv_sem=pair_sem.at[which],
            device_id=peer(4 if which == 0 else 2),
            device_id_type=MESH,
        )

    def pair_share(which, fresh):
        q = 3 - held(which) if fresh else held(which)
        return pltpu.make_async_remote_copy(
            src_ref=pair_buf.at[0, q],
            dst_ref=pair_buf.at[1, q],
            send_sem=pair_own_send.at[fresh, which],
            recv_sem=pair_own_sem.at[fresh, which],
            device_id=peer(1),
            device_id_type=MESH,
        )

    def pair_exchange():
        for which in range(2):
            q = held(which)
            here = pair_buf.at[0, q, pl.ds(pl.multiple_of(c * strip, strip), strip), :]
            pltpu.make_async_copy(here, here, pair_keep.at[which]).wait()

            @pl.loop(1, n_c)
            def _(d):
                plane = lax.rem(c + d, n_c)
                there = pair_buf.at[0, q, pl.ds(pl.multiple_of(plane * strip, strip), strip), :]
                pltpu.make_async_remote_copy(
                    src_ref=there,
                    dst_ref=there,
                    send_sem=pair_move_send.at[0, which],
                    recv_sem=pair_move_sem.at[which, plane],
                    device_id=peer(1),
                    device_id_type=MESH,
                ).wait_recv()

            pair_swap(which).start()
            pair_share(which, 0).start()

    def pair_arrive():
        for which in range(2):
            pair_swap(which).wait_recv()
            pair_share(which, 1).start()

    def pair_compute():
        for par in range(2):
            if par == 1:
                for fresh in range(2):
                    for which in range(2):
                        pair_share(which, fresh).wait_recv()
            side = core if par == 0 else 1 - core
            start = pl.multiple_of(side * wo_cols + rs_cols + t_cols, LANES)

            @pl.loop(0, 4)
            def _(q):
                acc[:, pl.ds(start, pair_cols)] += jnp.dot(
                    ctx_perm[q], pair_buf[par, q], preferred_element_type=jnp.float32
                )

    def gift(home, k):
        return tok.at[home, :, pl.ds(k * rs_cols, rs_cols)]

    def give(home, k, side):
        slot = jnp.where(home == c + 2 * side - 1, n_c * (1 - side) + home * side, home)
        return pltpu.make_async_remote_copy(
            src_ref=gift(home, k),
            dst_ref=rs_recv.at[slot, k],
            send_sem=give_send.at[home, k],
            recv_sem=give_sem.at[slot, k],
            device_id=(f, c + 2 * side - 1),
            device_id_type=MESH,
        )

    def got(slot, k):
        pltpu.make_async_remote_copy(
            src_ref=rs_recv.at[slot, k],
            dst_ref=rs_recv.at[slot, k],
            send_sem=give_send.at[0, k],
            recv_sem=give_sem.at[slot, k],
            device_id=peer(1),
            device_id_type=MESH,
        ).wait_recv()

    def rs_start():
        locals_in[5].wait()

        @pl.loop(0, n_f)
        def _(j):
            @pl.when(lax.rem(j, 2) == 1)
            def _():
                for h in range(HALVES):
                    arrived(2, j, 0, h)

            target = flip(j)
            cols = pl.ds(pl.multiple_of(lax.rem(target, 2) * rs_cols, LANES), rs_cols)
            tok[lax.div(target, 2), :, cols] = jnp.dot(
                qc[...], rs_buf[j], preferred_element_type=jnp.float32
            ).astype(jnp.bfloat16)

        @pl.when(c == 0)
        def _():
            for home in range(n_c - 1, 0, -1):
                for k in range(2):
                    give(home, k, 1).start()

        @pl.when(c == n_c - 1)
        def _():
            for home in range(n_c - 1):
                for k in range(2):
                    give(home, k, 0).start()

    def rs_pass(e, k):
        def add(home, side):
            got(home, k)
            cols = slice(k * rs_cols, (k + 1) * rs_cols)
            tok[home, :, cols] = (
                tok[home, :, cols].astype(jnp.float32) + rs_recv[home, k].astype(jnp.float32)
            ).astype(jnp.bfloat16)
            give(home, k, side).start()

        @pl.when(jnp.logical_and(c > 0, c + e < n_c))
        def _():
            add(c + e, 1)

        @pl.when(jnp.logical_and(c < n_c - 1, c - e >= 0))
        def _():
            add(c - e, 0)

    def take():
        for k in range(2):
            cols = slice(k * rs_cols, (k + 1) * rs_cols)
            place = out_cols(nw, k)
            acc[:, place] = tok[c, :, cols].astype(jnp.float32)

            @pl.when(c > 0)
            def _():
                got(c, k)
                acc[:, place] += rs_recv[c, k].astype(jnp.float32)

            @pl.when(c < n_c - 1)
            def _():
                got(n_c, k)
                acc[:, place] += rs_recv[n_c, k].astype(jnp.float32)

            out[:, place] = acc[:, place].astype(jnp.bfloat16)

    last_slot = 2 * min(m for m in masks if level[m] == levels)

    def shares(s, start, stop):
        @pl.loop(start, stop)
        def _(j):
            @pl.when(lax.rem(j, 2) == 1)
            def _():
                for h in range(HALVES):
                    arrived(1, j, s, h)

            share(j, s)

    def compute_early(i):
        kind, s = stream[i]
        if kind == 1 and levels > 1:
            shares(s, 0, 4)
            if levels == 2:
                shares(s, 4, last_slot)

    def compute(i):
        kind, s = stream[i]
        if kind == 0:
            @pl.loop(2, n_f)
            def _(j):
                @pl.when(lax.rem(j, 2) == 1)
                def _():
                    for h in range(HALVES):
                        arrived(0, j, s, h)

                q_part(j, s)

            attend(s)
            ctx_start(s)
            return
        if kind == 3:
            pair_compute()
            s = nw + 1
        else:
            shares(s, (last_slot if levels == 2 else 4) if levels > 1 else 0, n_f)
        for k in range(2):
            cols = out_cols(s, k)
            out[:, cols] = acc[:, cols].astype(jnp.bfloat16)

    def tok_copy(j):
        start = pl.multiple_of(flip(j) * depth, LANES)
        return pltpu.make_async_copy(tokens.at[:, pl.ds(start, depth)], tok.at[j], tok_sem.at[j])

    mine = pl.ds(pl.multiple_of(c * kv_cols, LANES), kv_cols)
    locals_in = [
        pltpu.make_async_copy(wq, wq_buf.at[0], own_sem.at[0]),
        pltpu.make_async_copy(kc.at[:, :, mine], k_buf.at[pl.ds(c * blk_dev, blk_dev)], own_sem.at[1]),
        pltpu.make_async_copy(vc.at[:, :, mine], v_buf.at[pl.ds(c * blk_dev, blk_dev)], own_sem.at[2]),
        pltpu.make_async_copy(cos_in, cos_ref, own_sem.at[3]),
        pltpu.make_async_copy(sin_in, sin_ref, own_sem.at[4]),
    ]
    if rs_cols:
        locals_in.append(pltpu.make_async_copy(wo.at[:, pl.ds(0, rs_cols)], rs_buf.at[0], own_sem.at[5]))

    barrier = pltpu.get_barrier_semaphore()

    def beside(sem, extra):
        for b in extra + [2 * b for b in bits]:
            pl.semaphore_signal(sem, inc=1, device_id=peer(b), device_id_type=MESH)

        @pl.when(c > 0)
        def _():
            pl.semaphore_signal(sem, inc=1, device_id=(f, c - 1), device_id_type=MESH)

        @pl.when(c < n_c - 1)
        def _():
            pl.semaphore_signal(sem, inc=1, device_id=(f, c + 1), device_id_type=MESH)

    near = len(bits) + jnp.where(c > 0, 1, 0) + jnp.where(c < n_c - 1, 1, 0)
    beside(barrier, [1])
    for copy in locals_in:
        copy.start()
    for j in range(n_f):
        tok_copy(j).start()
    acc[...] = jnp.zeros_like(acc)
    pl.semaphore_wait(barrier, near + 1)
    rounds = max(levels, n_c - 1) - 1

    def kv_start(d):
        @pl.when(c + d < n_c)
        def _():
            for which in range(2):
                kv_copy(which, d).start()

        @pl.when(c - d >= 0)
        def _():
            for which in range(2):
                kv_copy(which, n_c - d).start()

    def hops(lev):
        for m in masks:
            if level[m] == lev:
                hop_copy(lax.div(flip(2 * m), 2), chip).start()

    beside(round_sem.at[0], [])
    if pair_cols:
        for copy in pair_sources()[:4]:
            copy.start()
    hops(1)
    kv_start(1)
    for r in range(rounds):
        pl.semaphore_wait(round_sem.at[r], near)
        if r + 1 < rounds:
            beside(round_sem.at[r + 1], [])
        hops(r + 2)
        if r + 2 < n_c:
            kv_start(r + 2)
    if pair_cols:
        pair_forward()
    for i in range(AHEAD):
        directs(i)
    for s in range(nq):
        to_partner(0, s)
    if rs_cols:
        to_partner(2, 0)

    locals_in[0].wait()
    for j in range(n_f):
        tok_copy(j).wait()
    start_moves()
    if pair_cols:
        pair_rest()
    for s in range(nq):
        for h in range(HALVES):
            arrived(0, 1, s, h)

        @pl.loop(0, 2)
        def _(j):
            q_part(j, s)

    for copy in locals_in[1:5]:
        copy.wait()

    lag = levels - 1
    total = len(stream)
    done = {}
    queued = AHEAD

    def ctx_next(s):
        if done[s] < n_c:
            ctx_pass(s, done[s])
            done[s] += 1

    last = total + lag - 1
    if pair_cols:
        last = total - 1
    for step in range(last + 1):
        pass_level(step, 1)
        if pair_cols and step == last:
            compute(step)
        if pair_cols and step == 0:
            pair_far()
        i = step - lag
        while queued < total and queued <= step + AHEAD and not (rs_cols and step == nq - 1 and queued > nq):
            directs(queued)
            queued += 1
        for lev in range(2, levels):
            pass_level(step - lev + 1, lev)
        for s in range(nq):
            if s in done and not (rs_cols and s == nq - 1):
                ctx_next(s)
        if rs_cols and step == nq + 1:
            for k in range(2):
                for e in range(n_c - 2, 1, -1):
                    rs_pass(e, k)
                ctx_next(nq - 1)
        if i == first_wo:
            for s in range(nq):
                while done[s] < n_c:
                    ctx_next(s)
            for q in range(chips):
                for plane in range(n_c):
                    ctx_perm[q, :, plane * part:(plane + 1) * part] = ctx_all[
                        plane, :, q * part:(q + 1) * part
                    ]
        if i >= 0 and stream[i][0] != 2:
            if levels > 1:
                if not (pair_cols and step == last):
                    compute_early(i)
                pass_level(i, levels)
                if rs_cols and step == last:
                    take()
            if i == 0:
                @pl.loop(1, n_c)
                def _(d):
                    for which in range(2):
                        kv_wait(which, d)
            compute(i)
            if stream[i][0] == 0:
                done[stream[i][1]] = 1
            if i == nq - 1:
                if rs_cols:
                    pass_level(nq, 2)
                    rs_start()
                acc[...] = jnp.zeros_like(acc)
                ctx_next(nq - 1)
            if rs_cols and i == first_wo:
                for k in range(2):
                    rs_pass(1, k)
            if pair_cols and step == last - 1:
                compute_early(step)
        if step + 1 + AHEAD == max(first_wo, AHEAD + 1):
            wait_moves()
            for s in range(nw):
                to_partner(1, s)

    assert len(sent) == send_sem.shape[0]
    for copy in sent:
        copy.wait_send()

    @pl.loop(1, n_c)
    def _(d):
        for which in range(2):
            kv_copy(which, d).wait_send()

    for s in range(nq):
        ctx_drain(s)

    @pl.loop(0, chips)
    def _(q):
        @pl.when(q != chip)
        def _():
            hop_copy(q, chip).wait_send()

        home, _ = owner(q)

        @pl.when(home != c)
        def _():
            move(piece(chip), q).wait_send()

    if pair_cols:
        for copy in pair_sources():
            copy.wait_send()
        for which in range(2):
            for m in range(4):
                home, _, go = pair_move(m, which)

                @pl.when(home != c)
                def _():
                    go.wait_send()

            pair_swap(which).wait_send()
            for fresh in range(2):
                pair_share(which, fresh).wait_send()
    if rs_cols:
        for k in range(2):
            @pl.loop(0, n_c)
            def _(home):
                @pl.when(home != c)
                def _():
                    give(home, k, jnp.where(home > c, 1, 0)).wait_send()


def body(n_f, n_c, tokens, wq, wo, key_cache, value_cache, key_blocks):
    rows, width = tokens.shape
    depth = width // n_f
    qcols = wq.shape[1]
    cache = key_cache.shape[0]
    blk_dev = cache // BLOCK
    kv_cols = key_cache.shape[1] // n_c
    n_list = key_blocks.shape[2]
    cosine, sine = tables(rows, cache * n_c)
    nq = max(1, min(4, qcols // HEAD))
    ratio = n_f // n_c
    chips = n_f // 2
    part = wo.shape[0] // chips
    rs_cols = wo.shape[1] // 4 if ratio == 2 and n_f == chips * 2 == n_c * 2 and chips.bit_length() == 3 and wo.shape[1] % (4 * LANES) == 0 else 0
    pair_cols = rs_cols
    t_cols = wo.shape[1] - rs_cols - pair_cols
    moved = (part * n_c, t_cols * ratio // 2)
    if rs_cols:
        widths = [rs_cols] * (moved[1] // rs_cols)
    else:
        parts = max(1, min(4, moved[1] // LANES))
        widths = [moved[1] // parts] * parts
    cuts = tuple((sum(widths[:s]), w) for s, w in enumerate(widths))
    nw = len(cuts)
    strip = wo.shape[0] // 4
    pair_shape = (2, 4, n_c * strip, pair_cols) if pair_cols else (1, 1, 16, LANES)
    pair_hop_shape = (3, 2, strip, pair_cols) if pair_cols else (1, 1, 16, LANES)
    rs_shape = (wo.shape[0], rs_cols) if rs_cols else (16, LANES)
    share_shape = (n_c + 1, 2, rows, rs_cols) if rs_cols else (1, 1, 16, LANES)
    any_spec = pl.BlockSpec(memory_space=pl.ANY)
    bf16 = jnp.bfloat16
    f32 = jnp.float32
    dma = pltpu.SemaphoreType.DMA
    return pl.pallas_call(
        functools.partial(kernel, (n_f, n_c, nq, cuts, rs_cols, pair_cols)),
        out_shape=pltpu.VMEM((rows, width // n_c), bf16),
        in_specs=[pl.BlockSpec(memory_space=pltpu.SMEM)] + [any_spec] * 7,
        out_specs=pl.BlockSpec(memory_space=pltpu.VMEM),
        scratch_shapes=[
            pltpu.VMEM((n_f, rows, depth), bf16),
            pltpu.VMEM((n_f,) + wq.shape, bf16),
            pltpu.VMEM((n_f,) + moved, bf16),
            pltpu.VMEM((blk_dev * n_c, BLOCK, kv_cols), bf16),
            pltpu.VMEM((blk_dev * n_c, BLOCK, kv_cols), bf16),
            pltpu.VMEM((rows, max(qcols, width // n_c)), f32),
            pltpu.VMEM((rows, qcols), bf16),
            pltpu.VMEM((n_list * BLOCK, HEAD), bf16),
            pltpu.VMEM((n_list * BLOCK, HEAD), bf16),
            pltpu.VMEM((BLOCK, n_list * BLOCK), f32),
            pltpu.VMEM((n_c, rows, qcols), bf16),
            pltpu.VMEM((chips, rows, n_c * part), bf16),
            pltpu.VMEM((chips, part, t_cols), bf16),
            pltpu.VMEM((rows, HEAD), f32),
            pltpu.VMEM((rows, HEAD), f32),
            pltpu.VMEM((n_f if rs_cols else 1,) + rs_shape, bf16),
            pltpu.VMEM(share_shape, bf16),
            pltpu.VMEM(pair_shape, bf16),
            pltpu.VMEM(pair_hop_shape, bf16),
            dma((n_f,)),
            dma((6,)),
            dma(((nq + nw + (1 if rs_cols else 0)) * HALVES * (n_f - 1),)),
            dma((n_f, nq, HALVES)),
            dma((n_f, nw, HALVES)),
            dma((2, n_c)),
            dma((2, n_c)),
            dma((nq, n_c, 2)),
            dma((nq, n_c)),
            dma((chips,)),
            dma((ratio // 2, n_c)),
            dma((ratio // 2,)),
            dma((chips,)),
            dma((chips,)),
            pltpu.SemaphoreType.REGULAR((max(chips.bit_length() - 1, n_c - 1),)),
            dma((n_f, 1, HALVES)),
            dma((n_c, 2)),
            dma((n_c + 1, 2)),
            dma((6,)),
            dma((3, 2)),
            dma((4, 2)),
            dma((2, n_c)),
            dma((2,)),
            dma((2,)),
            dma((2,)),
            dma((2, 2)),
            dma((2, 2)),
        ],
        compiler_params=pltpu.CompilerParams(
            collective_id=0, has_side_effects=True, vmem_limit_bytes=67043328 - 2 * rows * width // n_c - 65536
        ),
    )(
        key_blocks,
        tokens,
        wq,
        wo,
        key_cache.reshape(blk_dev, BLOCK, key_cache.shape[1]),
        value_cache.reshape(blk_dev, BLOCK, value_cache.shape[1]),
        jnp.asarray(cosine, jnp.float32),
        jnp.asarray(sine, jnp.float32),
    )


def solution(mesh):
    in_specs = (
        P("fsdp", None),
        P("fsdp", "ctx"),
        P("ctx", "fsdp"),
        P(("fsdp", "ctx"), None),
        P(("fsdp", "ctx"), None),
        P("fsdp", None, None),
    )
    step = functools.partial(body, mesh.shape["fsdp"], mesh.shape["ctx"])
    return jax.shard_map(
        step, mesh=mesh, in_specs=in_specs, out_specs=P("fsdp", "ctx"), check_vma=False
    )
```
